32 devices in a mesh: slab: 4 (over z), tile: 8 (over y, x, core).
Axes of the slice: x: 2, y: 2, z: 4, core: 2. Of those that a mesh axis runs over, the one named last changes fastest.
Arguments:
- coarse: bfloat16 [192, 16, 32, 64], P(None, 'slab', 'tile'), may hold values from -6 to 6
- up_weight: bfloat16 [3, 3, 96, 192], replicated, may hold values from -0.15625 to 0.15625
- up_bias: float32 [96], replicated, may hold values from -3 to 3
- gain_one: float32 [96], replicated, may hold values from 0.1 to 1.9
- conv_one: bfloat16 [3, 3, 96, 288], replicated, may hold values from -0.125 to 0.125
- bias_one: float32 [96], replicated, may hold values from -3 to 3
- gain_two: float32 [96], replicated, may hold values from 0.1 to 1.9
- conv_two: bfloat16 [3, 3, 96, 288], replicated, may hold values from -0.125 to 0.125
- bias_two: float32 [96], replicated, may hold values from -3 to 3
Outputs:
- decoded: bfloat16 [96, 16, 64, 128], P(None, 'slab', 'tile')
The draws below stay inside these ranges and needn't reach their ends.
All inputs are finite; a program needn't handle non-finite values.
Results may differ from the reference program's by a relative error of at most 0.009.
Values may be sent and summed in bfloat16 or wider, within the bound.
A program may use at most 64 MiB of HBM per device.

```python
import jax
import jax.numpy as jnp
from jax import lax

COARSE_CH = 192
FINE_CH = 96
COLS = 128
FRAMES = 16
ROWS = 64


def steps_of(key, dims, shards, low, largest):
    def one(dim, shards_of):
        heights = jax.random.uniform(jax.random.fold_in(jax.random.fold_in(key, 6), dim), (shards_of,), jnp.float32, low / len(shards), largest / len(shards))
        return jnp.repeat(jnp.exp(heights), dims[dim] // shards_of).reshape((-1,) + (1,) * (len(dims) - dim - 1))

    loudness = one(*shards[0])
    for cut in shards[1:]:
        loudness = loudness * one(*cut)
    return loudness


def bell_draw(stream_key, shape, width, limit, pieces=(), dtype=jnp.bfloat16):
    values = width * jax.random.normal(stream_key, shape, jnp.float32)
    if pieces:
        values = values * steps_of(stream_key, shape, pieces, -0.22, 0.18)
    return jnp.clip(values, -limit, limit).astype(dtype)


def setup_inputs(seed: int = 0) -> dict:
    arg_keys = jax.random.split(jax.random.key(seed), 10)
    coarse = bell_draw(arg_keys[0], (COARSE_CH, FRAMES, ROWS // 2, COLS // 2), 1.0, 6.0, ((1, 4), (2, 8)))
    up_weight = bell_draw(arg_keys[1], (3, 3, FINE_CH, COARSE_CH), (9 * COARSE_CH) ** -0.5, 0.15625)
    up_bias = bell_draw(arg_keys[2], (FINE_CH,), 0.5, 3.0, (), jnp.float32)
    gain_one = jnp.clip(1.0 + 0.18 * jax.random.normal(arg_keys[3], (FINE_CH,), jnp.float32), 0.1, 1.9)
    conv_one = bell_draw(arg_keys[4], (3, 3, FINE_CH, 3 * FINE_CH), (27 * FINE_CH) ** -0.5, 0.125)
    bias_one = bell_draw(arg_keys[5], (FINE_CH,), 0.5, 3.0, (), jnp.float32)
    gain_two = jnp.clip(1.0 + 0.18 * jax.random.normal(arg_keys[6], (FINE_CH,), jnp.float32), 0.1, 1.9)
    conv_two = bell_draw(arg_keys[7], (3, 3, FINE_CH, 3 * FINE_CH), (27 * FINE_CH) ** -0.5, 0.125)
    bias_two = bell_draw(arg_keys[8], (FINE_CH,), 0.5, 3.0, (), jnp.float32)
    return {"coarse": coarse, "up_weight": up_weight, "up_bias": up_bias, "gain_one": gain_one, "conv_one": conv_one, "bias_one": bias_one, "gain_two": gain_two, "conv_two": conv_two, "bias_two": bias_two}


def norm_act(values, gain):
    meansq = lax.optimization_barrier(jnp.mean(values * values, axis=0, keepdims=True))
    scaled = values * lax.rsqrt(meansq + 1e-06) * gain[:, None, None, None]
    return (scaled * jax.nn.sigmoid(scaled)).astype(jnp.bfloat16)

def conv_frame(window, weight, bias):
    chans = window.shape[0]
    padded = jnp.pad(window, ((0, 0), (0, 0), (1, 1), (1, 1)))
    height = padded.shape[2] - 2
    breadth = padded.shape[3] - 2
    summed = jnp.zeros((weight.shape[2], height * breadth), jnp.float32)
    for t_tap in range(3):
        for h_tap in range(3):
            stacked = jnp.concatenate([padded[:, t_tap, h_tap:h_tap + height, w_tap:w_tap + breadth] for w_tap in range(3)], axis=0)
            summed = summed + jnp.dot(weight[t_tap, h_tap], stacked.reshape(3 * chans, -1), preferred_element_type=jnp.float32)
    return summed.reshape(-1, 1, height, breadth) + bias[:, None, None, None]

def plane_frame(padded, weight, bias):
    chans = padded.shape[0]
    height = padded.shape[1] - 2
    breadth = padded.shape[2] - 2
    summed = jnp.zeros((weight.shape[2], height * breadth), jnp.float32)
    for h_tap in range(3):
        for w_tap in range(3):
            window = padded[:, h_tap:h_tap + height, w_tap:w_tap + breadth].reshape(chans, -1)
            summed = summed + jnp.dot(weight[h_tap, w_tap], window, preferred_element_type=jnp.float32)
    return summed.reshape(-1, 1, height, breadth) + bias[:, None, None, None]

def reference(coarse, up_weight, up_bias, gain_one, conv_one, bias_one, gain_two, conv_two, bias_two):
    chans = up_weight.shape[2]
    height = coarse.shape[2] * 2
    breadth = coarse.shape[3] * 2
    frames_first = jnp.moveaxis(coarse, 1, 0)

    def advance(carry, frame):
        past_one, past_two = carry
        enlarged = jnp.repeat(jnp.repeat(frame, 2, axis=1), 2, axis=2)
        enlarged = jnp.pad(enlarged, ((0, 0), (1, 1), (1, 1)))
        upsampled = plane_frame(enlarged, up_weight, up_bias).astype(jnp.bfloat16)
        first_act = norm_act(upsampled.astype(jnp.float32), gain_one)
        window_one = jnp.concatenate([past_one, first_act], axis=1)
        hidden = conv_frame(window_one, conv_one, bias_one)
        second_act = norm_act(hidden, gain_two)
        window_two = jnp.concatenate([past_two, second_act], axis=1)
        result = upsampled.astype(jnp.float32) + conv_frame(window_two, conv_two, bias_two)
        return ((window_one[:, 1:], window_two[:, 1:]), result[:, 0].astype(jnp.bfloat16))
    start = (jnp.zeros((chans, 2, height, breadth), jnp.bfloat16), jnp.zeros((chans, 2, height, breadth), jnp.bfloat16))
    final, outputs = lax.scan(advance, start, frames_first)
    return jnp.moveaxis(outputs, 0, 1)
```

```python
import functools

import jax
import jax.numpy as jnp
from jax import lax
from jax.experimental import pallas as pl
from jax.experimental.pallas import tpu as pltpu
from jax.sharding import PartitionSpec as P

MESH = pl.DeviceIdType.MESH
F32 = jnp.float32
BF16 = jnp.bfloat16


def body(slabs, tiles, coarse, up_w, one_w, two_w, up_b, one_g, one_b, two_g, two_b, out,
         cbuf, wu, w1, w2, vecs, spread, part, ups, x1, acc1, x2, acc2, raw_u, raw_1, raw_2, load, near_send, near_recv, far_send, far_recv, hop_send, hop_recv):
    frames, _, _, cols = coarse.shape
    chans = out.shape[2]
    rows = out.shape[1]
    s = lax.axis_index("slab")
    t = lax.axis_index("tile")
    has_up, has_down = t > 0, t < tiles - 1
    has_prev, has_next = s > 0, s < slabs - 1
    sides = ((has_up, {"tile": t - 1}), (has_down, {"tile": t + 1}), (has_prev, {"slab": s - 1}), (has_next, {"slab": s + 1}))

    def remote(src, dst, send, recv, who):
        return pltpu.make_async_remote_copy(
            src_ref=src, dst_ref=dst, send_sem=send, recv_sem=recv, device_id=who, device_id_type=MESH)

    loads = [pltpu.make_async_copy(src, dst, load.at[n])
             for n, (src, dst) in enumerate(((up_w, raw_u), (one_w, raw_1), (two_w, raw_2)))]
    for copy in loads:
        copy.start()

    barrier = pltpu.get_barrier_semaphore()
    for there, who in sides:
        @pl.when(there)
        def _():
            pl.semaphore_signal(barrier, inc=1, device_id=who, device_id_type=MESH)
    to_up = [remote(coarse.at[f, 0], cbuf.at[frames + f, 3], near_send.at[f, 0], near_recv.at[f, 0], {"tile": t - 1}) for f in range(frames)]
    to_down = [remote(coarse.at[f, 1], cbuf.at[frames + f, 0], near_send.at[f, 1], near_recv.at[f, 1], {"tile": t + 1}) for f in range(frames)]
    far = [remote(coarse.at[f], cbuf.at[f, pl.ds(1, 2)], far_send.at[f], far_recv.at[f], {"slab": s + 1}) for f in range(frames)]
    hop_up = [remote(cbuf.at[f, 1], cbuf.at[f, 3], hop_send.at[f, 0], hop_recv.at[f, 0], {"tile": t - 1}) for f in range(frames)]
    hop_down = [remote(cbuf.at[f, 2], cbuf.at[f, 0], hop_send.at[f, 1], hop_recv.at[f, 1], {"tile": t + 1}) for f in range(frames)]

    for f in range(frames):
        cbuf[frames + f, 1] = coarse[f, 0]
        cbuf[frames + f, 2] = coarse[f, 1]

    rim = jnp.zeros(cbuf.shape[2:], BF16)

    @pl.when(jnp.logical_not(has_up))
    def _():
        for f in range(frames):
            cbuf[frames + f, 0] = rim

    @pl.when(jnp.logical_not(has_down))
    def _():
        for f in range(frames):
            cbuf[frames + f, 3] = rim

    @pl.when(jnp.logical_or(jnp.logical_not(has_prev), jnp.logical_not(has_up)))
    def _():
        for f in range(frames):
            cbuf[f, 0] = rim

    @pl.when(jnp.logical_or(jnp.logical_not(has_prev), jnp.logical_not(has_down)))
    def _():
        for f in range(frames):
            cbuf[f, 3] = rim

    @pl.when(jnp.logical_not(has_prev))
    def _():
        for f in range(frames):
            cbuf[f, 1] = rim
            cbuf[f, 2] = rim

    half = cols // 2
    lane = lax.broadcasted_iota(jnp.int32, (cols, cols), 0)
    col = lax.broadcasted_iota(jnp.int32, (cols, cols), 1)
    for j in range(2):
        hit = lane == j * half + lax.shift_right_arithmetic(col, 1)
        spread[:, j * cols:(j + 1) * cols] = jnp.where(hit, 1.0, 0.0).astype(BF16)

    for n, vec in enumerate((up_b, one_g, one_b, two_g, two_b)):
        vecs[n] = jnp.transpose(jnp.broadcast_to(vec[...], (cols, chans)))
    pl.semaphore_wait(barrier, sum(there.astype(jnp.int32) for there, _ in sides))
    for f in reversed(range(frames)):
        pl.when(has_up)(to_up[f].start)
        pl.when(has_down)(to_down[f].start)
        pl.when(has_next)(far[f].start)

    loads[0].wait()
    up = [jnp.concatenate([raw_u[a, b] for b in range(3)], axis=1).astype(F32) for a in range(3)]
    for q, mix in enumerate((up[2], up[1] + up[2], up[0] + up[1], up[0])):
        wu[q * chans:(q + 1) * chans] = mix.astype(BF16)
    for n, raw, w in ((1, raw_1, w1), (2, raw_2, w2)):
        loads[n].wait()
        for tap in range(3):
            w[tap * chans:(tap + 1) * chans] = jnp.concatenate([raw[tap, a] for a in range(3)], axis=1)

    row_col = lax.broadcasted_iota(jnp.int32, (1, cols), 1)

    def norm_act(values, gain):
        meansq = jnp.mean(values * values, axis=0, keepdims=True)
        y = values * lax.rsqrt(meansq + 1e-06) * gain
        return y / (1.0 + jnp.exp(-y))

    def shifts(v):
        left = jnp.where(row_col == 0, 0.0, pltpu.roll(v, 1, 1)).astype(BF16)
        right = jnp.where(row_col == cols - 1, 0.0, pltpu.roll(v, cols - 1, 1)).astype(BF16)
        return left, v.astype(BF16), right

    def put(ref, f, r, act):
        pieces = shifts(act)

        def store():
            for b in range(3):
                ref[f, r, pl.ds(b * chans, chans)] = pieces[b]
        return store

    def run(trips, *steps):
        for i in range(trips):
            for store in [store for step in steps for store in step(i)]:
                store()

    top_keep = jnp.where(has_up, 1.0, 0.0)
    bottom_keep = jnp.where(has_down, 1.0, 0.0)
    past_keep = jnp.where(has_prev, 1.0, 0.0)

    def row_keep(r, low, high):
        if isinstance(r, int):
            return top_keep if r < low else bottom_keep if r >= high else 1.0
        return jnp.where(r < low, top_keep, jnp.where(r >= high, bottom_keep, 1.0))

    def expand(f):
        slot = f % frames

        def step(pair):
            wide = jnp.dot(cbuf[f, pair], spread[...], preferred_element_type=F32)
            near = [jnp.concatenate(shifts(wide[:, j * cols:(j + 1) * cols]), axis=0) for j in range(2)]
            lo = chans if pair == 0 else 0
            hi = 3 * chans if pair == 3 else 4 * chans
            got = jnp.dot(wu[lo:hi], jnp.concatenate(near, axis=1), preferred_element_type=F32)

            def store():
                part[slot, 2 * pair, lo:hi] = got[:, :cols]
                part[slot, 2 * pair + 1, lo:hi] = got[:, cols:]
            return [store]
        return step

    def finish(f, i):
        slot = f % frames
        even = part[slot, i, pl.ds(chans, chans)] + part[slot, i - 1, pl.ds(3 * chans, chans)]
        odd = part[slot, i, pl.ds(2 * chans, chans)] + part[slot, i + 1, pl.ds(0, chans)]
        stores = []
        for j, total in enumerate((even, odd)):
            r = 2 * (i - 1) + j
            value = (total + vecs[0]).astype(BF16)
            act = norm_act(value.astype(F32), vecs[1])
            keep = row_keep(r, 2, rows + 2)
            if f < frames:
                keep = keep * past_keep
            stores.append(put(x1, f, r, act * keep))
            if f >= frames:
                def keep_value(r=r, value=value):
                    ups[f - frames, r] = value
                stores.append(keep_value)
        return stores

    turns = ((1,), (2, 3), (4,), (5, 6))

    def level(old, new):
        for k in range(4):
            stores = [store for i in turns[k] for store in finish(old, i)]
            if new is not None:
                stores += expand(new)(k)
            for store in stores:
                store()

    def conv(x, w, acc, f, last, start_of, done):
        taps = [tap for tap in range(3) if 0 <= f - tap <= last]
        lo, hi = taps[0], taps[-1] + 1

        def step(p):
            r = 2 * p
            lines = [x[f, r + a] for a in range(4)]
            rhs = jnp.concatenate([jnp.concatenate([lines[a], lines[a + 1]], axis=1) for a in range(3)], axis=0)
            got = jnp.dot(w[pl.ds(lo * chans, (hi - lo) * chans)], rhs, preferred_element_type=F32)

            def store():
                for tap in taps:
                    n = f - tap
                    for j in range(2):
                        mine = got[(tap - lo) * chans:(tap - lo + 1) * chans, j * cols:(j + 1) * cols]
                        total = mine + (start_of(n, r + j) if tap == 2 else acc[n, r + j])
                        if tap == 0 and done is not None:
                            done(n, r + j, total)
                        else:
                            acc[n, r + j] = total
            return [store]
        return step

    mids = frames + 2

    def conv_a(f):
        return conv(x1, w1, acc1, f, mids - 1, lambda n, r: vecs[2], None)

    def finished(n, r, total):
        out[n, r] = total.astype(BF16)

    def conv_b(f):
        return conv(x2, w2, acc2, f, frames - 1, lambda n, r: ups[n, r + 2].astype(F32) + vecs[4], finished)

    def second(n, r):
        act = norm_act(acc1[n, r], vecs[3])
        keep = row_keep(r, 1, rows + 1)
        if n < 2:
            keep = keep * past_keep
        return [put(x2, n, r, act * keep)]

    def second_two(n):
        return lambda p: second(n, 2 * p) + second(n, 2 * p + 1)

    newest = 2 * frames - 1

    def lone(f, pairs):
        for pair in pairs:
            for store in expand(f)(pair):
                store()

    def arrived(f):
        pl.when(has_down)(to_up[f - frames].wait_recv)
        pl.when(has_up)(to_down[f - frames].wait_recv)

    def relay(f):
        @pl.when(has_prev)
        def _():
            far[f].wait_recv()
            pl.when(has_up)(hop_up[f].start)
            pl.when(has_down)(hop_down[f].start)

    def landed(f):
        @pl.when(has_prev)
        def _():
            pl.when(has_down)(hop_up[f].wait_recv)
            pl.when(has_up)(hop_down[f].wait_recv)

    wide_pairs = (rows + 2) // 2
    for f in reversed(range(frames, 2 * frames)):
        lone(f, (1, 2))
    for f in reversed(range(frames, 2 * frames)):
        arrived(f)
        lone(f, (0, 3))
        level(f, None)
        if f + 1 < mids:
            run(wide_pairs, second_two(f + 1), conv_a(f))
        else:
            run(wide_pairs, conv_a(f))
        if f < newest:
            relay(f + 1 - frames)
    run(rows // 2, second_two(frames), conv_b(frames + 1))
    run(1, lambda p: second_two(frames)(rows // 2))
    relay(0)
    landed(frames - 1)
    run(rows // 2, conv_b(frames), expand(frames - 1))
    for f in reversed(range(frames)):
        if f > 0:
            landed(f - 1)
        level(f, f - 1 if f > 0 else None)
        run(wide_pairs, conv_a(f))
        run(wide_pairs, second_two(f))
        run(rows // 2, conv_b(f))

    for f in range(frames):
        pl.when(has_up)(to_up[f].wait_send)
        pl.when(has_down)(to_down[f].wait_send)
    for f in range(frames):
        pl.when(has_next)(far[f].wait_send)
        pl.when(jnp.logical_and(has_prev, has_up))(hop_up[f].wait_send)
        pl.when(jnp.logical_and(has_prev, has_down))(hop_down[f].wait_send)


def shards(slabs, tiles, coarse, up_weight, up_bias, gain_one, conv_one, bias_one, gain_two, conv_two, bias_two):
    deep, frames, lines, half = coarse.shape
    chans = up_weight.shape[2]
    rows, cols = 2 * lines, 2 * half
    packed = coarse.transpose(1, 2, 0, 3).reshape(frames, lines // 2, 2, deep, half)
    packed = packed.transpose(0, 1, 3, 2, 4).reshape(frames, lines // 2, deep, cols)
    row = lambda vec: vec.reshape(1, chans)
    vmem = pl.BlockSpec(memory_space=pltpu.VMEM)
    got = pl.pallas_call(
        functools.partial(body, slabs, tiles),
        out_shape=jax.ShapeDtypeStruct((frames, rows, chans, cols), BF16),
        in_specs=[vmem] + [pl.BlockSpec(memory_space=pltpu.HBM)] * 3 + [vmem] * 5,
        out_specs=vmem,
        scratch_shapes=[
            pltpu.VMEM((2 * frames, 4, deep, cols), BF16),
            pltpu.VMEM((4 * chans, 3 * deep), BF16),
            pltpu.VMEM((3 * chans, 9 * chans), BF16),
            pltpu.VMEM((3 * chans, 9 * chans), BF16),
            pltpu.VMEM((5, chans, cols), F32),
            pltpu.VMEM((cols, 2 * cols), BF16),
            pltpu.VMEM((frames, 8, 4 * chans, cols), F32),
            pltpu.VMEM((frames, rows + 4, chans, cols), BF16),
            pltpu.VMEM((2 * frames, rows + 4, 3 * chans, cols), BF16),
            pltpu.VMEM((frames + 2, rows + 2, chans, cols), F32),
            pltpu.VMEM((frames + 2, rows + 2, 3 * chans, cols), BF16),
            pltpu.VMEM((frames, rows, chans, cols), F32),
            pltpu.VMEM(up_weight.shape, BF16),
            pltpu.VMEM(conv_one.shape, BF16),
            pltpu.VMEM(conv_two.shape, BF16),
            pltpu.SemaphoreType.DMA((3,)),
            pltpu.SemaphoreType.DMA((frames, 2)),
            pltpu.SemaphoreType.DMA((frames, 2)),
            pltpu.SemaphoreType.DMA((frames,)),
            pltpu.SemaphoreType.DMA((frames,)),
            pltpu.SemaphoreType.DMA((frames, 2)),
            pltpu.SemaphoreType.DMA((frames, 2)),
        ],
        compiler_params=pltpu.CompilerParams(collective_id=0, has_side_effects=True, vmem_limit_bytes=60 * 2**20),
    )(packed, up_weight, conv_one, conv_two, row(up_bias), row(gain_one), row(bias_one), row(gain_two), row(bias_two))
    return got.transpose(2, 0, 1, 3)


def solution(mesh):
    return jax.shard_map(
        functools.partial(shards, mesh.shape["slab"], mesh.shape["tile"]),
        mesh=mesh,
        in_specs=(P(None, "slab", "tile", None), P(), P(), P(), P(), P(), P(), P(), P()),
        out_specs=P(None, "slab", "tile", None),
        check_vma=False,
    )
```

```python
import functools

import jax
import jax.numpy as jnp
from jax import lax
from jax.experimental import pallas as pl
from jax.experimental.pallas import tpu as pltpu
from jax.sharding import PartitionSpec as P

MESH = pl.DeviceIdType.MESH
F32 = jnp.float32
BF16 = jnp.bfloat16


def body(slabs, tiles, coarse, up_w, one_w, two_w, up_b, one_g, one_b, two_g, two_b, out,
         native, cbuf, we, wo, w1, w2, vecs, merge, vals, x1, acc1, x2, acc2, raw_u, raw_1, raw_2, fetch, load,
         near_send, near_recv, far_send, far_recv, hop_send, hop_recv):
    frames = coarse.shape[0]
    chans = out.shape[2]
    rows = out.shape[1]
    cols = cbuf.shape[3]
    half = cols // 2
    s = lax.axis_index("slab")
    t = lax.axis_index("tile")
    has_up, has_down = t > 0, t < tiles - 1
    has_prev, has_next = s > 0, s < slabs - 1
    sides = ((has_next, {"slab": s + 1}), (has_prev, {"slab": s - 1}), (has_up, {"tile": t - 1}), (has_down, {"tile": t + 1}))

    def remote(src, dst, send, recv, who):
        return pltpu.make_async_remote_copy(
            src_ref=src, dst_ref=dst, send_sem=send, recv_sem=recv, device_id=who, device_id_type=MESH)

    fetches = [pltpu.make_async_copy(coarse.at[f], native.at[f], fetch.at[f]) for f in range(frames)]
    for copy in reversed(fetches):
        copy.start()

    barrier = pltpu.get_barrier_semaphore()
    for there, who in sides:
        @pl.when(there)
        def _():
            pl.semaphore_signal(barrier, inc=1, device_id=who, device_id_type=MESH)

    loads = [pltpu.make_async_copy(src, dst, load.at[n])
             for n, (src, dst) in enumerate(((up_w, raw_u), (one_w, raw_1), (two_w, raw_2)))]
    for copy in loads:
        copy.start()

    to_up = [remote(cbuf.at[frames + f, 1], cbuf.at[frames + f, 3], near_send.at[f, 0], near_recv.at[f, 0], {"tile": t - 1}) for f in range(frames)]
    to_down = [remote(cbuf.at[frames + f, 2], cbuf.at[frames + f, 0], near_send.at[f, 1], near_recv.at[f, 1], {"tile": t + 1}) for f in range(frames)]
    far = [remote(cbuf.at[frames + f, pl.ds(1, 2)], cbuf.at[f, pl.ds(1, 2)], far_send.at[f], far_recv.at[f], {"slab": s + 1}) for f in range(frames)]
    hop_up = [remote(cbuf.at[f, 1], cbuf.at[f, 3], hop_send.at[f, 0], hop_recv.at[f, 0], {"tile": t - 1}) for f in range(frames)]
    hop_down = [remote(cbuf.at[f, 2], cbuf.at[f, 0], hop_send.at[f, 1], hop_recv.at[f, 1], {"tile": t + 1}) for f in range(frames)]

    rim = jnp.zeros(cbuf.shape[2:], BF16)

    @pl.when(jnp.logical_not(has_up))
    def _():
        for f in range(frames):
            cbuf[frames + f, 0] = rim

    @pl.when(jnp.logical_not(has_down))
    def _():
        for f in range(frames):
            cbuf[frames + f, 3] = rim

    @pl.when(jnp.logical_or(jnp.logical_not(has_prev), jnp.logical_not(has_up)))
    def _():
        for f in range(frames):
            cbuf[f, 0] = rim

    @pl.when(jnp.logical_or(jnp.logical_not(has_prev), jnp.logical_not(has_down)))
    def _():
        for f in range(frames):
            cbuf[f, 3] = rim

    @pl.when(jnp.logical_not(has_prev))
    def _():
        for f in range(frames):
            cbuf[f, 1] = rim
            cbuf[f, 2] = rim

    for f in reversed(range(frames)):
        fetches[f].wait()
        turned = jnp.transpose(native[f])
        cbuf[frames + f, 1] = turned[:, :cols]
        cbuf[frames + f, 2] = turned[:, cols:]

    pl.semaphore_wait(barrier, sum(there.astype(jnp.int32) for there, _ in sides))
    for f in reversed(range(frames)):
        pl.when(has_next)(far[f].start)
        pl.when(has_up)(to_up[f].start)
        pl.when(has_down)(to_down[f].start)

    line = lax.broadcasted_iota(jnp.int32, (2 * cols, 2 * cols), 0)
    col = lax.broadcasted_iota(jnp.int32, (2 * cols, 2 * cols), 1)
    inner = jnp.bitwise_and(col, cols - 1)
    place = jnp.bitwise_and(col, cols) + lax.shift_right_arithmetic(inner, 1) + half * jnp.bitwise_and(inner, 1)
    merge[...] = jnp.where(line == place, 1.0, 0.0).astype(BF16)

    for n, vec in enumerate((up_b, one_g, one_b, two_g, two_b)):
        vecs[n] = jnp.transpose(jnp.broadcast_to(vec[...], (cols, chans)))

    loads[0].wait()
    for phase in range(2):
        lines = []
        for near_row in range(2):
            picks = ((0, 1), (2,)) if phase == 0 else ((0,), (1, 2))
            taps = picks[near_row]
            lines.append([sum(raw_u[a, b].astype(F32) for a in taps) for b in range(3)])
        for w, pick in ((we, lambda u: (u[0], u[1] + u[2])), (wo, lambda u: (u[0] + u[1], u[2]))):
            w[phase * chans:(phase + 1) * chans] = jnp.concatenate(
                [piece for u in lines for piece in pick(u)], axis=1).astype(BF16)
    for n, raw, w in ((1, raw_1, w1), (2, raw_2, w2)):
        loads[n].wait()
        for tap in range(3):
            w[tap * chans:(tap + 1) * chans] = jnp.concatenate([raw[tap, a] for a in range(3)], axis=1)

    def lanes_of(depth):
        return lax.broadcasted_iota(jnp.int32, (depth, cols), 1)

    deep = cbuf.shape[2]
    low_deep = lanes_of(deep) < half
    open_left = jnp.bitwise_and(lanes_of(deep), half - 1) != 0
    open_right = jnp.bitwise_and(lanes_of(deep), half - 1) != half - 1
    low = lanes_of(chans) < half
    first = lanes_of(chans) == 0
    last = lanes_of(chans) == cols - 1
    none_deep = jnp.zeros((deep, cols), BF16)
    none = jnp.zeros((chans, cols), BF16)

    def norm_act(values, gain, keep):
        meansq = jnp.mean(values * values, axis=0, keepdims=True)
        y = values * (lax.rsqrt(meansq + 1e-06) * (0.5 * keep)) * gain
        return y + y * jnp.tanh(y)

    def put(ref, f, r, act):
        mid = act.astype(BF16)
        cross = pltpu.roll(mid, half, 1)
        left = jnp.where(first, none, jnp.where(low, pltpu.roll(mid, half + 1, 1), cross))
        right = jnp.where(last, none, jnp.where(low, cross, pltpu.roll(mid, half - 1, 1)))

        def store():
            for b, piece in enumerate((left, mid, right)):
                ref[f, r, pl.ds(b * chans, chans)] = piece
        return store

    def run(trips, *steps):
        for i in range(trips):
            for store in [store for step in steps for store in step(i)]:
                store()

    top_keep = jnp.where(has_up, 1.0, 0.0)
    bottom_keep = jnp.where(has_down, 1.0, 0.0)
    past_keep = jnp.where(has_prev, 1.0, 0.0)

    def row_keep(r, lo, hi):
        return top_keep if r < lo else bottom_keep if r >= hi else 1.0

    def windows(f, p):
        here = cbuf[f, p]
        swap = pltpu.roll(here, half, 1)
        if p < 3:
            after = cbuf[f, p + 1]
            below = jnp.where(low_deep, swap, pltpu.roll(after, half, 1))
            below_swap = jnp.where(low_deep, after, here)
        else:
            below, below_swap = swap, here

        def to_left(v):
            return jnp.where(open_left, pltpu.roll(v, 1, 1), none_deep)

        def to_right(v):
            return jnp.where(open_right, pltpu.roll(v, cols - 1, 1), none_deep)
        even = jnp.concatenate([to_left(here), here, to_left(below), below], axis=0)
        odd = jnp.concatenate([swap, to_right(swap), below_swap, to_right(below_swap)], axis=0)
        return even, odd

    def grow(*jobs):
        cut = [windows(f, p) for f, p in jobs]
        even, odd = [jnp.dot(w[...], jnp.concatenate([c[k] for c in cut], axis=1), preferred_element_type=F32)
                     for k, w in enumerate((we, wo))]
        stores = []
        for k, (f, p) in enumerate(jobs):
            for phase in range(2):
                e = even[phase * chans:(phase + 1) * chans, k * cols:(k + 1) * cols] + vecs[0]
                o = odd[phase * chans:(phase + 1) * chans, k * cols:(k + 1) * cols] + vecs[0]
                for side in range(2):
                    r = 2 * (2 * p + side) - 1 + phase
                    if 0 <= r < rows + 4:
                        if side == 0:
                            value = jnp.where(lanes_of(chans) < half, e, o).astype(BF16)
                        else:
                            value = pltpu.roll(jnp.where(lanes_of(chans) < half, o, e).astype(BF16), half, 1)

                        def store(f=f, r=r, value=value):
                            vals[f, r] = value
                        stores.append(store)
        return stores

    def growing(*works):
        return lambda i: grow(*works[i]) if i < len(works) else []

    def finish(f, r):
        keep = row_keep(r, 2, rows + 2)
        if f < frames:
            keep = keep * past_keep
        return put(x1, f, r, norm_act(vals[f, r].astype(F32), vecs[1], keep))

    def finishing(f, trips):
        each = -(-(rows + 4) // trips)
        return lambda i: [finish(f, r) for r in range(i * each, min((i + 1) * each, rows + 4))]

    def conv(x, w, acc, f, newest_out, start_of, done):
        taps = [tap for tap in range(3) if 0 <= f - tap <= newest_out]
        lo, hi = taps[0], taps[-1] + 1

        def step(p):
            r = 2 * p
            lines = [x[f, r + a] for a in range(4)]
            rhs = jnp.concatenate([jnp.concatenate([lines[a], lines[a + 1]], axis=1) for a in range(3)], axis=0)
            got = jnp.dot(w[pl.ds(lo * chans, (hi - lo) * chans)], rhs, preferred_element_type=F32)

            def store():
                for tap in taps:
                    n = f - tap
                    totals = []
                    for j in range(2):
                        mine = got[(tap - lo) * chans:(tap - lo + 1) * chans, j * cols:(j + 1) * cols]
                        totals.append(mine + (start_of(n, r + j) if tap == 2 else acc[n, r + j]))
                    if tap == 0 and done is not None:
                        done(n, r, totals)
                    else:
                        for j in range(2):
                            acc[n, r + j] = totals[j]
            return [store]
        return step

    mids = frames + 2

    def conv_a(f):
        return conv(x1, w1, acc1, f, mids - 1, lambda n, r: vecs[2], None)

    def finished(n, r, totals):
        flat = jnp.concatenate([total.astype(BF16) for total in totals], axis=1)
        wide = jnp.dot(flat, merge[...], preferred_element_type=F32).astype(BF16)
        for j in range(2):
            out[n, r + j] = wide[:, j * cols:(j + 1) * cols]

    def conv_b(f):
        return conv(x2, w2, acc2, f, frames - 1, lambda n, r: vals[frames + n, r + 2].astype(F32) + vecs[4], finished)

    def second(n, r):
        keep = row_keep(r, 1, rows + 1)
        if n < 2:
            keep = keep * past_keep
        return put(x2, n, r, norm_act(acc1[n, r], vecs[3], keep))

    def second_two(n):
        return lambda p: [second(n, 2 * p), second(n, 2 * p + 1)] if 2 * p < rows + 2 else []

    def arrived(f):
        pl.when(has_down)(to_up[f - frames].wait_recv)
        pl.when(has_up)(to_down[f - frames].wait_recv)

    def relay(f):
        @pl.when(has_prev)
        def _():
            far[f].wait_recv()
            pl.when(has_up)(hop_up[f].start)
            pl.when(has_down)(hop_down[f].start)

    def landed(f):
        @pl.when(has_prev)
        def _():
            pl.when(has_down)(hop_up[f].wait_recv)
            pl.when(has_up)(hop_down[f].wait_recv)

    wide_pairs = (rows + 2) // 2
    pairs = rows // 2
    n = 2 * frames
    run(2, growing(((n - 1, 1), (n - 2, 1)), ((n - 3, 1), (n - 4, 1))))
    arrived(n - 1)
    arrived(n - 2)
    run(3, growing(((n - 1, 0), (n - 1, 2)), ((n - 2, 0), (n - 2, 2)), ((n - 1, 3), (n - 2, 3))))
    arrived(n - 3)
    arrived(n - 4)
    run(3, growing(((n - 3, 0), (n - 3, 2)), ((n - 4, 0), (n - 4, 2)), ((n - 3, 3), (n - 4, 3))), finishing(n - 1, 3))
    run(wide_pairs, conv_a(n - 1), finishing(n - 2, wide_pairs))
    relay(3)
    run(wide_pairs, conv_a(n - 2), finishing(n - 3, wide_pairs))
    relay(2)
    run(wide_pairs, conv_a(n - 3), finishing(n - 4, wide_pairs))
    run(wide_pairs, conv_a(n - 4), second_two(5))
    relay(1)
    run(wide_pairs, second_two(4), lambda p: conv_b(5)(p) if p < pairs else [])
    landed(3)
    landed(2)
    run(4, conv_b(4), growing(((3, 0), (3, 1)), ((3, 2), (3, 3)), ((2, 0), (2, 1)), ((2, 2), (2, 3))))
    relay(0)
    run(3, finishing(3, 3))
    run(wide_pairs, conv_a(3), finishing(2, wide_pairs))
    run(wide_pairs, conv_a(2), second_two(3))
    landed(1)
    run(wide_pairs, lambda p: conv_b(3)(p) if p < pairs else [], second_two(2), growing(((1, 0), (1, 1)), ((1, 2), (1, 3))))
    run(4, conv_b(2), finishing(1, 4))
    run(wide_pairs, conv_a(1))
    landed(0)
    run(wide_pairs, second_two(1), growing(((0, 0), (0, 1)), ((0, 2), (0, 3))))
    run(4, conv_b(1), finishing(0, 4))
    run(wide_pairs, conv_a(0))
    run(wide_pairs, second_two(0))
    run(4, conv_b(0))

    for f in range(frames):
        pl.when(has_up)(to_up[f].wait_send)
        pl.when(has_down)(to_down[f].wait_send)
        pl.when(has_next)(far[f].wait_send)
        pl.when(jnp.logical_and(has_prev, has_up))(hop_up[f].wait_send)
        pl.when(jnp.logical_and(has_prev, has_down))(hop_down[f].wait_send)


def shards(slabs, tiles, coarse, up_weight, up_bias, gain_one, conv_one, bias_one, gain_two, conv_two, bias_two):
    deep, frames, lines, half = coarse.shape
    chans = up_weight.shape[2]
    rows, cols = 2 * lines, 2 * half
    native = coarse.transpose(1, 2, 3, 0).reshape(frames, lines * half, deep)
    row = lambda vec: vec.reshape(1, chans)
    vmem = pl.BlockSpec(memory_space=pltpu.VMEM)
    far_away = pl.BlockSpec(memory_space=pl.ANY)
    got = pl.pallas_call(
        functools.partial(body, slabs, tiles),
        out_shape=jax.ShapeDtypeStruct((frames, rows, chans, cols), BF16),
        in_specs=[far_away] * 4 + [vmem] * 5,
        out_specs=vmem,
        scratch_shapes=[
            pltpu.VMEM((frames, lines * half, deep), BF16),
            pltpu.VMEM((2 * frames, 4, deep, cols), BF16),
            pltpu.VMEM((2 * chans, 4 * deep), BF16),
            pltpu.VMEM((2 * chans, 4 * deep), BF16),
            pltpu.VMEM((3 * chans, 9 * chans), BF16),
            pltpu.VMEM((3 * chans, 9 * chans), BF16),
            pltpu.VMEM((5, chans, cols), F32),
            pltpu.VMEM((2 * cols, 2 * cols), BF16),
            pltpu.VMEM((2 * frames, rows + 4, chans, cols), BF16),
            pltpu.VMEM((2 * frames, rows + 4, 3 * chans, cols), BF16),
            pltpu.VMEM((frames + 2, rows + 2, chans, cols), F32),
            pltpu.VMEM((frames + 2, rows + 2, 3 * chans, cols), BF16),
            pltpu.VMEM((frames, rows, chans, cols), F32),
            pltpu.VMEM(up_weight.shape, BF16),
            pltpu.VMEM(conv_one.shape, BF16),
            pltpu.VMEM(conv_two.shape, BF16),
            pltpu.SemaphoreType.DMA((frames,)),
            pltpu.SemaphoreType.DMA((3,)),
            pltpu.SemaphoreType.DMA((frames, 2)),
            pltpu.SemaphoreType.DMA((frames, 2)),
            pltpu.SemaphoreType.DMA((frames,)),
            pltpu.SemaphoreType.DMA((frames,)),
            pltpu.SemaphoreType.DMA((frames, 2)),
            pltpu.SemaphoreType.DMA((frames, 2)),
        ],
        compiler_params=pltpu.CompilerParams(collective_id=0, has_side_effects=True, vmem_limit_bytes=60 * 2**20),
    )(native, up_weight, conv_one, conv_two, row(up_bias), row(gain_one), row(bias_one), row(gain_two), row(bias_two))
    return got.transpose(2, 0, 1, 3)


def solution(mesh):
    return jax.shard_map(
        functools.partial(shards, mesh.shape["slab"], mesh.shape["tile"]),
        mesh=mesh,
        in_specs=(P(None, "slab", "tile", None), P(), P(), P(), P(), P(), P(), P(), P()),
        out_specs=P(None, "slab", "tile", None),
        check_vma=False,
    )
```

```python
import functools

import jax
import jax.numpy as jnp
from jax import lax
from jax.experimental import pallas as pl
from jax.experimental.pallas import tpu as pltpu
from jax.sharding import PartitionSpec as P

MESH = pl.DeviceIdType.MESH
F32 = jnp.float32
BF16 = jnp.bfloat16


def body(slabs, tiles, coarse, up_w, one_w, two_w, up_b, one_g, one_b, two_g, two_b, out,
         native, cbuf, we, wo, w1, w2, vecs, merge, vals, x1, acc1, x2, acc2, raw_u, raw_1, raw_2, spread, staged, fetch, load, leave,
         near_send, near_recv, far_send, far_recv, hop_send, hop_recv):
    frames = coarse.shape[0]
    chans, _, rows, _ = out.shape
    cols = cbuf.shape[3]
    half = cols // 2
    s = lax.axis_index("slab")
    t = lax.axis_index("tile")
    has_up, has_down = t > 0, t < tiles - 1
    has_prev, has_next = s > 0, s < slabs - 1
    sides = ((has_next, {"slab": s + 1}), (has_prev, {"slab": s - 1}), (has_up, {"tile": t - 1}), (has_down, {"tile": t + 1}))

    def remote(src, dst, send, recv, who):
        return pltpu.make_async_remote_copy(
            src_ref=src, dst_ref=dst, send_sem=send, recv_sem=recv, device_id=who, device_id_type=MESH)

    fetches = [pltpu.make_async_copy(coarse.at[f], native.at[f], fetch.at[f]) for f in range(frames)]
    for copy in reversed(fetches):
        copy.start()

    barrier = pltpu.get_barrier_semaphore()
    for there, who in sides:
        @pl.when(there)
        def _():
            pl.semaphore_signal(barrier, inc=1, device_id=who, device_id_type=MESH)

    loads = [pltpu.make_async_copy(src, dst, load.at[n])
             for n, (src, dst) in enumerate(((up_w, raw_u), (one_w, raw_1), (two_w, raw_2)))]
    for copy in loads:
        copy.start()

    to_up = [remote(cbuf.at[frames + f, 1], cbuf.at[frames + f, 3], near_send.at[f, 0], near_recv.at[f, 0], {"tile": t - 1}) for f in range(frames)]
    to_down = [remote(cbuf.at[frames + f, 2], cbuf.at[frames + f, 0], near_send.at[f, 1], near_recv.at[f, 1], {"tile": t + 1}) for f in range(frames)]
    far = [remote(cbuf.at[frames + f, pl.ds(1, 2)], cbuf.at[f, pl.ds(1, 2)], far_send.at[f], far_recv.at[f], {"slab": s + 1}) for f in range(frames)]
    hop_up = [remote(cbuf.at[f, 1], cbuf.at[f, 3], hop_send.at[f, 0], hop_recv.at[f, 0], {"tile": t - 1}) for f in range(frames)]
    hop_down = [remote(cbuf.at[f, 2], cbuf.at[f, 0], hop_send.at[f, 1], hop_recv.at[f, 1], {"tile": t + 1}) for f in range(frames)]

    rim = jnp.zeros(cbuf.shape[2:], BF16)

    @pl.when(jnp.logical_not(has_up))
    def _():
        for f in range(frames):
            cbuf[frames + f, 0] = rim

    @pl.when(jnp.logical_not(has_down))
    def _():
        for f in range(frames):
            cbuf[frames + f, 3] = rim

    @pl.when(jnp.logical_or(jnp.logical_not(has_prev), jnp.logical_not(has_up)))
    def _():
        for f in range(frames):
            cbuf[f, 0] = rim

    @pl.when(jnp.logical_or(jnp.logical_not(has_prev), jnp.logical_not(has_down)))
    def _():
        for f in range(frames):
            cbuf[f, 3] = rim

    @pl.when(jnp.logical_not(has_prev))
    def _():
        for f in range(frames):
            cbuf[f, 1] = rim
            cbuf[f, 2] = rim

    line = lax.broadcasted_iota(jnp.int32, (2 * cols, 2 * cols), 0)
    col = lax.broadcasted_iota(jnp.int32, (2 * cols, 2 * cols), 1)
    inner = jnp.bitwise_and(col, cols - 1)
    place = jnp.bitwise_and(col, cols) + lax.shift_right_arithmetic(inner, 1) + half * jnp.bitwise_and(inner, 1)
    merge[...] = jnp.where(line == place, 1.0, 0.0).astype(BF16)

    for n, vec in enumerate((up_b, one_g, one_b, two_g, two_b)):
        vecs[n] = jnp.transpose(jnp.broadcast_to(vec[...], (cols, chans)))

    for f in reversed(range(frames)):
        fetches[f].wait()
        turned = jnp.transpose(native[f])
        cbuf[frames + f, 1] = turned[:, :cols]
        cbuf[frames + f, 2] = turned[:, cols:]

    pl.semaphore_wait(barrier, sum(there.astype(jnp.int32) for there, _ in sides))
    for f in reversed(range(frames)):
        pl.when(has_up)(to_up[f].start)
        pl.when(has_down)(to_down[f].start)
    for f in reversed(range(frames)):
        pl.when(has_next)(far[f].start)

    loads[0].wait()
    for phase in range(2):
        lines = []
        for near_row in range(2):
            picks = ((0, 1), (2,)) if phase == 0 else ((0,), (1, 2))
            taps = picks[near_row]
            lines.append([sum(raw_u[a, b].astype(F32) for a in taps) for b in range(3)])
        for w, pick in ((we, lambda u: (u[0], u[1] + u[2])), (wo, lambda u: (u[0] + u[1], u[2]))):
            w[phase * chans:(phase + 1) * chans] = jnp.concatenate(
                [piece for u in lines for piece in pick(u)], axis=1).astype(BF16)
    for n, raw, w in ((1, raw_1, w1), (2, raw_2, w2)):
        loads[n].wait()
        for tap in range(3):
            w[tap * chans:(tap + 1) * chans] = jnp.concatenate([raw[tap, a] for a in range(3)], axis=1)

    def lanes_of(depth):
        return lax.broadcasted_iota(jnp.int32, (depth, cols), 1)

    deep = cbuf.shape[2]
    low_deep = lanes_of(deep) < half
    open_left = jnp.bitwise_and(lanes_of(deep), half - 1) != 0
    open_right = jnp.bitwise_and(lanes_of(deep), half - 1) != half - 1
    low = lanes_of(chans) < half
    first = lanes_of(chans) == 0
    last = lanes_of(chans) == cols - 1
    none_deep = jnp.zeros((deep, cols), BF16)
    none = jnp.zeros((chans, cols), BF16)

    def norm_act(values, gain, keep):
        meansq = jnp.mean(values * values, axis=0, keepdims=True)
        y = values * (lax.rsqrt(meansq + 1e-06) * (0.5 * keep)) * gain
        return y + y * jnp.tanh(y)

    def put(ref, f, r, act):
        mid = act.astype(BF16)
        cross = pltpu.roll(mid, half, 1)
        left = jnp.where(first, none, jnp.where(low, pltpu.roll(mid, half + 1, 1), cross))
        right = jnp.where(last, none, jnp.where(low, cross, pltpu.roll(mid, half - 1, 1)))

        def store():
            for b, piece in enumerate((left, mid, right)):
                ref[f, r, pl.ds(b * chans, chans)] = piece
        return store

    def run(trips, *steps):
        for i in range(trips):
            for store in [store for step in steps for store in step(i)]:
                store()

    top_keep = jnp.where(has_up, 1.0, 0.0)
    bottom_keep = jnp.where(has_down, 1.0, 0.0)
    past_keep = jnp.where(has_prev, 1.0, 0.0)

    def row_keep(r, lo, hi):
        return top_keep if r < lo else bottom_keep if r >= hi else 1.0

    def windows(f, p):
        here = cbuf[f, p]
        swap = pltpu.roll(here, half, 1)
        if p < 3:
            after = cbuf[f, p + 1]
            below = jnp.where(low_deep, swap, pltpu.roll(after, half, 1))
            below_swap = jnp.where(low_deep, after, here)
        else:
            below, below_swap = swap, here

        def to_left(v):
            return jnp.where(open_left, pltpu.roll(v, 1, 1), none_deep)

        def to_right(v):
            return jnp.where(open_right, pltpu.roll(v, cols - 1, 1), none_deep)
        even = jnp.concatenate([to_left(here), here, to_left(below), below], axis=0)
        odd = jnp.concatenate([swap, to_right(swap), below_swap, to_right(below_swap)], axis=0)
        return even, odd

    def grow(*jobs):
        cut = [windows(f, p) for f, p in jobs]
        even, odd = [jnp.dot(w[...], jnp.concatenate([c[k] for c in cut], axis=1), preferred_element_type=F32)
                     for k, w in enumerate((we, wo))]
        stores = []
        for k, (f, p) in enumerate(jobs):
            for phase in range(2):
                e = even[phase * chans:(phase + 1) * chans, k * cols:(k + 1) * cols] + vecs[0]
                o = odd[phase * chans:(phase + 1) * chans, k * cols:(k + 1) * cols] + vecs[0]
                for side in range(2):
                    r = 2 * (2 * p + side) - 1 + phase
                    if 0 <= r < rows + 4:
                        if side == 0:
                            value = jnp.where(lanes_of(chans) < half, e, o).astype(BF16)
                        else:
                            value = pltpu.roll(jnp.where(lanes_of(chans) < half, o, e).astype(BF16), half, 1)

                        def store(f=f, r=r, value=value):
                            vals[f, r] = value
                        stores.append(store)
        return stores

    def growing(*works):
        return lambda i: grow(*works[i]) if i < len(works) else []

    def finish(f, r):
        keep = row_keep(r, 2, rows + 2)
        if f < frames:
            keep = keep * past_keep
        return put(x1, f, r, norm_act(vals[f, r].astype(F32), vecs[1], keep))

    def finishing(f, trips):
        left = [r for r in range(rows + 4) if f < frames or not 3 <= r < 7]
        each = -(-len(left) // trips)
        return lambda i: [finish(f, r) for r in left[i * each:(i + 1) * each]]

    def conv(x, w, acc, f, newest_out, start_of, done):
        taps = [tap for tap in range(3) if 0 <= f - tap <= newest_out]
        lo, hi = taps[0], taps[-1] + 1

        def step(p):
            r = 2 * p
            lines = [x[f, r + a] for a in range(4)]
            rhs = jnp.concatenate([jnp.concatenate([lines[a], lines[a + 1]], axis=1) for a in range(3)], axis=0)
            got = jnp.dot(w[pl.ds(lo * chans, (hi - lo) * chans)], rhs, preferred_element_type=F32)

            def store():
                for tap in taps:
                    n = f - tap
                    totals = []
                    for j in range(2):
                        mine = got[(tap - lo) * chans:(tap - lo + 1) * chans, j * cols:(j + 1) * cols]
                        totals.append(mine + (start_of(n, r + j) if tap == 2 else acc[n, r + j]))
                    if tap == 0 and done is not None:
                        done(n, r, totals)
                    else:
                        for j in range(2):
                            acc[n, r + j] = totals[j]
            return [store]
        return step

    mids = frames + 2

    def conv_a(f):
        return conv(x1, w1, acc1, f, mids - 1, lambda n, r: vecs[2], None)

    def finished(n, r, totals):
        flat = jnp.concatenate([total.astype(BF16) for total in totals], axis=1)
        wide = jnp.dot(flat, merge[...], preferred_element_type=F32)
        for j in range(2):
            spread[n % 2, pl.ds(r + j, chans, stride=rows)] = wide[:, j * cols:(j + 1) * cols]

    leaving = [pltpu.make_async_copy(staged.at[n], out.at[:, n], leave.at[n]) for n in range(frames)]

    def emit(n):
        staged[n] = spread[n % 2].reshape(chans, rows, cols).astype(BF16)
        leaving[n].start()

    def conv_b(f):
        return conv(x2, w2, acc2, f, frames - 1, lambda n, r: vals[frames + n, r + 2].astype(F32) + vecs[4], finished)

    def second(n, r):
        keep = row_keep(r, 1, rows + 1)
        if n < 2:
            keep = keep * past_keep
        return put(x2, n, r, norm_act(acc1[n, r], vecs[3], keep))

    def second_two(n):
        return lambda p: [second(n, 2 * p), second(n, 2 * p + 1)] if 2 * p < rows + 2 else []

    def arrived(f):
        pl.when(has_down)(to_up[f - frames].wait_recv)
        pl.when(has_up)(to_down[f - frames].wait_recv)

    def relay(f):
        @pl.when(has_prev)
        def _():
            far[f].wait_recv()
            pl.when(has_up)(hop_up[f].start)
            pl.when(has_down)(hop_down[f].start)

    def landed(f):
        @pl.when(has_prev)
        def _():
            pl.when(has_down)(hop_up[f].wait_recv)
            pl.when(has_up)(hop_down[f].wait_recv)

    wide_pairs = (rows + 2) // 2
    pairs = rows // 2
    n = 2 * frames
    run(2, growing(((n - 1, 1), (n - 2, 1)), ((n - 3, 1), (n - 4, 1))))
    run(4, lambda i: [finish(n - 1 - i, r) for r in range(3, 7)])
    arrived(n - 1)
    arrived(n - 2)
    run(3, growing(((n - 1, 0), (n - 1, 2)), ((n - 2, 0), (n - 2, 2)), ((n - 1, 3), (n - 2, 3))))
    arrived(n - 3)
    arrived(n - 4)
    run(3, growing(((n - 3, 0), (n - 3, 2)), ((n - 4, 0), (n - 4, 2)), ((n - 3, 3), (n - 4, 3))), finishing(n - 1, 3))
    run(wide_pairs, conv_a(n - 1), finishing(n - 2, wide_pairs))
    relay(3)
    run(wide_pairs, conv_a(n - 2), finishing(n - 3, wide_pairs))
    relay(2)
    run(wide_pairs, conv_a(n - 3), finishing(n - 4, wide_pairs))
    run(wide_pairs, conv_a(n - 4), second_two(5))
    relay(1)
    run(wide_pairs, second_two(4), lambda p: conv_b(5)(p) if p < pairs else [])
    landed(3)
    landed(2)
    run(4, conv_b(4), growing(((3, 0), (3, 1)), ((3, 2), (3, 3)), ((2, 0), (2, 1)), ((2, 2), (2, 3))))
    relay(0)
    run(3, finishing(3, 3))
    run(wide_pairs, conv_a(3), finishing(2, wide_pairs))
    run(wide_pairs, conv_a(2), second_two(3))
    landed(1)
    run(wide_pairs, lambda p: conv_b(3)(p) if p < pairs else [], second_two(2), growing(((1, 0), (1, 1)), ((1, 2), (1, 3))))
    emit(3)
    run(4, conv_b(2), finishing(1, 4))
    emit(2)
    run(wide_pairs, conv_a(1))
    landed(0)
    run(wide_pairs, second_two(1), growing(((0, 0), (0, 1)), ((0, 2), (0, 3))))
    run(4, conv_b(1), finishing(0, 4))
    emit(1)
    run(wide_pairs, conv_a(0))
    run(wide_pairs, second_two(0))
    run(4, conv_b(0))
    emit(0)

    for f in range(frames):
        leaving[f].wait()
        pl.when(has_up)(to_up[f].wait_send)
        pl.when(has_down)(to_down[f].wait_send)
        pl.when(has_next)(far[f].wait_send)
        pl.when(jnp.logical_and(has_prev, has_up))(hop_up[f].wait_send)
        pl.when(jnp.logical_and(has_prev, has_down))(hop_down[f].wait_send)


def shards(slabs, tiles, coarse, up_weight, up_bias, gain_one, conv_one, bias_one, gain_two, conv_two, bias_two):
    deep, frames, lines, half = coarse.shape
    chans = up_weight.shape[2]
    rows, cols = 2 * lines, 2 * half
    native = coarse.transpose(1, 2, 3, 0).reshape(frames, lines * half, deep)
    row = lambda vec: vec.reshape(1, chans)
    vmem = pl.BlockSpec(memory_space=pltpu.VMEM)
    far_away = pl.BlockSpec(memory_space=pl.ANY)
    return pl.pallas_call(
        functools.partial(body, slabs, tiles),
        out_shape=jax.ShapeDtypeStruct((chans, frames, rows, cols), BF16),
        in_specs=[far_away] * 4 + [vmem] * 5,
        out_specs=far_away,
        scratch_shapes=[
            pltpu.VMEM((frames, lines * half, deep), BF16),
            pltpu.VMEM((2 * frames, 4, deep, cols), BF16),
            pltpu.VMEM((2 * chans, 4 * deep), BF16),
            pltpu.VMEM((2 * chans, 4 * deep), BF16),
            pltpu.VMEM((3 * chans, 9 * chans), BF16),
            pltpu.VMEM((3 * chans, 9 * chans), BF16),
            pltpu.VMEM((5, chans, cols), F32),
            pltpu.VMEM((2 * cols, 2 * cols), BF16),
            pltpu.VMEM((2 * frames, rows + 4, chans, cols), BF16),
            pltpu.VMEM((2 * frames, rows + 4, 3 * chans, cols), BF16),
            pltpu.VMEM((frames + 2, rows + 2, chans, cols), F32),
            pltpu.VMEM((frames + 2, rows + 2, 3 * chans, cols), BF16),
            pltpu.VMEM((frames, rows, chans, cols), F32),
            pltpu.VMEM(up_weight.shape, BF16),
            pltpu.VMEM(conv_one.shape, BF16),
            pltpu.VMEM(conv_two.shape, BF16),
            pltpu.VMEM((2, chans * rows, cols), F32),
            pltpu.VMEM((frames, chans, rows, cols), BF16),
            pltpu.SemaphoreType.DMA((frames,)),
            pltpu.SemaphoreType.DMA((3,)),
            pltpu.SemaphoreType.DMA((frames,)),
            pltpu.SemaphoreType.DMA((frames, 2)),
            pltpu.SemaphoreType.DMA((frames, 2)),
            pltpu.SemaphoreType.DMA((frames,)),
            pltpu.SemaphoreType.DMA((frames,)),
            pltpu.SemaphoreType.DMA((frames, 2)),
            pltpu.SemaphoreType.DMA((frames, 2)),
        ],
        compiler_params=pltpu.CompilerParams(collective_id=0, has_side_effects=True, vmem_limit_bytes=60 * 2**20),
    )(native, up_weight, conv_one, conv_two, row(up_bias), row(gain_one), row(bias_one), row(gain_two), row(bias_two))


def solution(mesh):
    return jax.shard_map(
        functools.partial(shards, mesh.shape["slab"], mesh.shape["tile"]),
        mesh=mesh,
        in_specs=(P(None, "slab", "tile", None), P(), P(), P(), P(), P(), P(), P(), P()),
        out_specs=P(None, "slab", "tile", None),
        check_vma=False,
    )
```

```python
import functools

import jax
import jax.numpy as jnp
from jax import lax
from jax.experimental import pallas as pl
from jax.experimental.pallas import tpu as pltpu
from jax.sharding import PartitionSpec as P

MESH = pl.DeviceIdType.MESH
F32 = jnp.float32
BF16 = jnp.bfloat16


def body(slabs, tiles, coarse, up_w, one_w, two_w, up_b, one_g, one_b, two_g, two_b, out,
         native, cbuf, we, wo, w1, w2, vecs, merge, vals, x1, acc1, x2, acc2, raw_u, raw_1, raw_2, spread, staged, fetch, load, leave,
         near_send, near_recv, far_send, far_recv, hop_send, hop_recv):
    frames = coarse.shape[0]
    chans, _, rows, _ = out.shape
    cols = cbuf.shape[3]
    half = cols // 2
    s = lax.axis_index("slab")
    t = lax.axis_index("tile")
    up, down = lax.rem(t + tiles - 1, tiles), lax.rem(t + 1, tiles)
    has_prev, has_next = s > 0, s < slabs - 1

    def remote(src, dst, send, recv, who):
        return pltpu.make_async_remote_copy(
            src_ref=src, dst_ref=dst, send_sem=send, recv_sem=recv, device_id=who, device_id_type=MESH)

    fetches = [pltpu.make_async_copy(coarse.at[f], native.at[f], fetch.at[f]) for f in range(frames)]
    for copy in reversed(fetches):
        copy.start()

    barrier = pltpu.get_barrier_semaphore()
    for who in ({"tile": up}, {"tile": down}):
        pl.semaphore_signal(barrier, inc=1, device_id=who, device_id_type=MESH)
    for there, who in ((has_next, s + 1), (has_prev, s - 1)):
        @pl.when(there)
        def _():
            pl.semaphore_signal(barrier, inc=1, device_id={"slab": who}, device_id_type=MESH)

    loads = [pltpu.make_async_copy(src, dst, load.at[n])
             for n, (src, dst) in enumerate(((up_w, raw_u), (one_w, raw_1), (two_w, raw_2)))]
    for copy in loads:
        copy.start()

    to_up = [remote(cbuf.at[frames + f, 1], cbuf.at[frames + f, 3], near_send.at[f, 0], near_recv.at[f, 0], {"tile": up}) for f in range(frames)]
    to_down = [remote(cbuf.at[frames + f, 2], cbuf.at[frames + f, 0], near_send.at[f, 1], near_recv.at[f, 1], {"tile": down}) for f in range(frames)]
    far = [remote(cbuf.at[frames + f, pl.ds(1, 2)], cbuf.at[f, pl.ds(1, 2)], far_send.at[f], far_recv.at[f], {"slab": s + 1}) for f in range(frames)]
    hop_up = [remote(cbuf.at[f, 1], cbuf.at[f, 3], hop_send.at[f, 0], hop_recv.at[f, 0], {"tile": up}) for f in range(frames)]
    hop_down = [remote(cbuf.at[f, 2], cbuf.at[f, 0], hop_send.at[f, 1], hop_recv.at[f, 1], {"tile": down}) for f in range(frames)]

    line = lax.broadcasted_iota(jnp.int32, (2 * cols, 2 * cols), 0)
    col = lax.broadcasted_iota(jnp.int32, (2 * cols, 2 * cols), 1)
    inner = jnp.bitwise_and(col, cols - 1)
    place = jnp.bitwise_and(col, cols) + lax.shift_right_arithmetic(inner, 1) + half * jnp.bitwise_and(inner, 1)
    merge[...] = jnp.where(line == place, 1.0, 0.0).astype(BF16)

    for n, vec in enumerate((up_b, one_g, one_b, two_g, two_b)):
        vecs[n] = jnp.transpose(jnp.broadcast_to(vec[...], (cols, chans)))

    for f in reversed(range(frames)):
        fetches[f].wait()
        turned = jnp.transpose(native[f])
        cbuf[frames + f, 1] = turned[:, :cols]
        cbuf[frames + f, 2] = turned[:, cols:]

    @pl.when(jnp.logical_not(has_prev))
    def _():
        for f in range(frames):
            for q in range(4):
                cbuf[f, q] = jnp.zeros(cbuf.shape[2:], BF16)

    pl.semaphore_wait(barrier, 2 + has_prev.astype(jnp.int32) + has_next.astype(jnp.int32))
    for f in reversed(range(frames)):
        to_up[f].start()
        to_down[f].start()

    @pl.when(has_next)
    def _():
        for f in reversed(range(frames)):
            far[f].start()

    loads[0].wait()
    for phase in range(2):
        lines = []
        for near_row in range(2):
            picks = ((0, 1), (2,)) if phase == 0 else ((0,), (1, 2))
            taps = picks[near_row]
            lines.append([sum(raw_u[a, b].astype(F32) for a in taps) for b in range(3)])
        for w, pick in ((we, lambda u: (u[0], u[1] + u[2])), (wo, lambda u: (u[0] + u[1], u[2]))):
            w[phase * chans:(phase + 1) * chans] = jnp.concatenate(
                [piece for u in lines for piece in pick(u)], axis=1).astype(BF16)
    for n, raw, w in ((1, raw_1, w1), (2, raw_2, w2)):
        loads[n].wait()
        for tap in range(3):
            w[tap * chans:(tap + 1) * chans] = jnp.concatenate([raw[tap, a] for a in range(3)], axis=1)

    def lanes_of(depth):
        return lax.broadcasted_iota(jnp.int32, (depth, cols), 1)

    deep = cbuf.shape[2]
    low_deep = lanes_of(deep) < half
    open_left = jnp.bitwise_and(lanes_of(deep), half - 1) != 0
    open_right = jnp.bitwise_and(lanes_of(deep), half - 1) != half - 1
    low = lanes_of(chans) < half
    first = lanes_of(chans) == 0
    last = lanes_of(chans) == cols - 1
    none_deep = jnp.zeros((deep, cols), BF16)
    none = jnp.zeros((chans, cols), BF16)

    def norm_act(values, gain, keep):
        meansq = jnp.mean(values * values, axis=0, keepdims=True)
        y = values * (lax.rsqrt(meansq + 1e-06) * (0.5 * keep)) * gain
        return y + y * jnp.tanh(y)

    def put(ref, f, r, act):
        mid = act.astype(BF16)
        cross = pltpu.roll(mid, half, 1)
        left = jnp.where(first, none, jnp.where(low, pltpu.roll(mid, half + 1, 1), cross))
        right = jnp.where(last, none, jnp.where(low, cross, pltpu.roll(mid, half - 1, 1)))

        def store():
            for b, piece in enumerate((left, mid, right)):
                ref[f, r, pl.ds(b * chans, chans)] = piece
        return store

    def run(trips, *steps):
        for i in range(trips):
            for store in [store for step in steps for store in step(i)]:
                store()

    top_keep = jnp.where(t > 0, 1.0, 0.0)
    bottom_keep = jnp.where(t < tiles - 1, 1.0, 0.0)
    past_keep = jnp.where(s > 0, 1.0, 0.0)
    top_mask = jnp.full((deep, cols), top_keep, F32).astype(BF16)
    bottom_mask = jnp.full((deep, cols), bottom_keep, F32).astype(BF16)

    def row_keep(r, lo, hi):
        return top_keep if r < lo else bottom_keep if r >= hi else 1.0

    def windows(f, kind):
        def lines(q):
            got = cbuf[f, q]
            return got * top_mask if q == 0 else got * bottom_mask if q == 3 else got

        def between(q):
            one, two = lines(q), lines(q + 1)
            return (jnp.where(low_deep, pltpu.roll(one, half, 1), pltpu.roll(two, half, 1)),
                    jnp.where(low_deep, two, one))
        if kind < 2:
            here, (below, below_swap) = lines(kind), between(kind)
            swap = pltpu.roll(here, half, 1)
        elif kind == 2:
            here = below_swap = lines(2)
            swap = below = pltpu.roll(here, half, 1)
        else:
            (here, swap), below = between(2), lines(3)
            below_swap = pltpu.roll(below, half, 1)

        def to_left(v):
            return jnp.where(open_left, pltpu.roll(v, 1, 1), none_deep)

        def to_right(v):
            return jnp.where(open_right, pltpu.roll(v, cols - 1, 1), none_deep)
        even = jnp.concatenate([to_left(here), here, to_left(below), below], axis=0)
        odd = jnp.concatenate([swap, to_right(swap), below_swap, to_right(below_swap)], axis=0)
        return even, odd

    def grow(*jobs):
        cut = [windows(f, p) for f, p in jobs]
        even, odd = [jnp.dot(w[...], jnp.concatenate([c[k] for c in cut], axis=1), preferred_element_type=F32)
                     for k, w in enumerate((we, wo))]
        stores = []
        for k, (f, p) in enumerate(jobs):
            for phase in range(2):
                e = even[phase * chans:(phase + 1) * chans, k * cols:(k + 1) * cols] + vecs[0]
                o = odd[phase * chans:(phase + 1) * chans, k * cols:(k + 1) * cols] + vecs[0]
                for side in range(1 if p == 2 else 2):
                    r = 2 * ((0, 2, 4, 5)[p] + side) - 1 + phase
                    if 0 <= r < rows + 4:
                        if side == 0:
                            value = jnp.where(lanes_of(chans) < half, e, o).astype(BF16)
                        else:
                            value = pltpu.roll(jnp.where(lanes_of(chans) < half, o, e).astype(BF16), half, 1)

                        def store(f=f, r=r, value=value):
                            vals[f, r] = value
                        stores.append(store)
        return stores

    def growing(*works):
        return lambda i: grow(*works[i]) if i < len(works) else []

    def finish(f, r):
        keep = row_keep(r, 2, rows + 2)
        if f < frames:
            keep = keep * past_keep
        return put(x1, f, r, norm_act(vals[f, r].astype(F32), vecs[1], keep))

    inner = list(range(3, rows + 1))
    outer = [r for r in range(rows + 4) if r not in inner]

    def finishing(f, lines, trips):
        each = -(-len(lines) // trips)
        return lambda i: [finish(f, r) for r in lines[i * each:(i + 1) * each]]

    def conv(x, w, acc, f, newest_out, pairs, start_of, done):
        taps = [tap for tap in range(3) if 0 <= f - tap <= newest_out]
        lo, hi = taps[0], taps[-1] + 1

        def step(p):
            if p >= len(pairs):
                return []
            rhs = jnp.concatenate(
                [jnp.concatenate([x[f, r + a] for r in pairs[p]], axis=1) for a in range(3)], axis=0)
            got = jnp.dot(w[pl.ds(lo * chans, (hi - lo) * chans)], rhs, preferred_element_type=F32)

            def store():
                for tap in taps:
                    n = f - tap
                    totals = []
                    for j, r in enumerate(pairs[p]):
                        mine = got[(tap - lo) * chans:(tap - lo + 1) * chans, j * cols:(j + 1) * cols]
                        totals.append(mine + (start_of(n, r) if tap == 2 else acc[n, r]))
                    if tap == 0 and done is not None:
                        done(n, pairs[p], totals)
                    else:
                        for r, total in zip(pairs[p], totals):
                            acc[n, r] = total
            return [store]
        return step

    mids = frames + 2

    early = [(r, r + 1) for r in range(3, rows - 1, 2)]
    late = [(1, 2), (rows - 1, rows), (0, rows + 1)]

    def conv_a(f, pairs=early + late):
        return conv(x1, w1, acc1, f, mids - 1, pairs, lambda n, r: vecs[2], None)

    def finished(n, pair, totals):
        flat = jnp.concatenate([total.astype(BF16) for total in totals], axis=1)
        wide = jnp.dot(flat, merge[...], preferred_element_type=F32)
        for j, r in enumerate(pair):
            spread[n % 2, pl.ds(r, chans, stride=rows)] = wide[:, j * cols:(j + 1) * cols]

    leaving = [pltpu.make_async_copy(staged.at[n], out.at[:, n], leave.at[n]) for n in range(frames)]

    def emit(n):
        staged[n] = spread[n % 2].reshape(chans, rows, cols).astype(BF16)
        leaving[n].start()

    def conv_b(f):
        return conv(x2, w2, acc2, f, frames - 1, [(r, r + 1) for r in range(0, rows, 2)], lambda n, r: vals[frames + n, r + 2].astype(F32) + vecs[4], finished)

    def second(n, r):
        keep = row_keep(r, 1, rows + 1)
        if n < 2:
            keep = keep * past_keep
        return put(x2, n, r, norm_act(acc1[n, r], vecs[3], keep))

    def second_two(n):
        return lambda p: [second(n, 2 * p), second(n, 2 * p + 1)] if 2 * p < rows + 2 else []

    def arrived(f):
        to_up[f - frames].wait_recv()
        to_down[f - frames].wait_recv()

    def relay(*sent):
        for f in sent:
            far[f].wait_recv()
            hop_up[f].start()
            hop_down[f].start()

    def landed(*sent):
        for f in sent:
            hop_up[f].wait_recv()
            hop_down[f].wait_recv()

    def middle(f):
        return growing(((f, 1), (f, 2)))

    def rim(f):
        return growing(((f, 0), (f, 3)))

    wide_pairs = (rows + 2) // 2
    lines = list(range(rows + 4))
    n = 2 * frames
    run(1, middle(n - 1))
    run(1, middle(n - 2), finishing(n - 1, inner, 1))
    run(2, middle(n - 3), conv_a(n - 1, early), finishing(n - 2, inner, 2))
    run(2, middle(n - 4), conv_a(n - 2, early), finishing(n - 3, inner, 2))
    run(2, conv_a(n - 3, early), finishing(n - 4, inner, 2))
    run(2, conv_a(n - 4, early))
    def rims(f, *others):
        run(1, rim(f), *others)

    arrived(n - 1)
    arrived(n - 2)
    rims(n - 1)
    rims(n - 2, finishing(n - 1, outer, 1))
    run(3, conv_a(n - 1, late), finishing(n - 2, outer, 3))
    arrived(n - 3)
    arrived(n - 4)
    rims(n - 3)
    run(3, conv_a(n - 2, late), finishing(n - 3, outer, 3), rim(n - 4))
    run(3, conv_a(n - 3, late), finishing(n - 4, outer, 3))
    pl.when(has_prev)(lambda: relay(3, 2))
    run(wide_pairs, conv_a(n - 4, late), second_two(5), middle(3))
    run(wide_pairs, second_two(4), conv_b(5), finishing(3, inner, 2), middle(2))
    run(4, conv_b(4), conv_a(3, early), finishing(2, inner, 3))
    run(3, conv_a(2, early))

    @pl.when(has_prev)
    def _():
        landed(3, 2)
        relay(1, 0)
    run(2, rim(3), middle(1))
    run(3, rim(2), finishing(3, outer, 3))
    run(3, conv_a(3, late), finishing(2, outer, 3), middle(0))
    run(wide_pairs, conv_a(2, late), second_two(3), finishing(1, inner, 3))
    run(wide_pairs, conv_b(3), second_two(2), finishing(0, inner, 4))
    run(4, conv_b(2), conv_a(1, early))
    emit(3)
    run(3, conv_a(0, early))
    emit(2)
    pl.when(has_prev)(lambda: landed(1, 0))
    run(1, rim(1))
    run(1, rim(0), finishing(1, outer, 1))
    run(3, conv_a(1, late), finishing(0, outer, 3))
    run(wide_pairs, conv_a(0, late), second_two(1))
    run(wide_pairs, conv_b(1), second_two(0))
    emit(1)
    run(4, conv_b(0))
    emit(0)

    for f in range(frames):
        leaving[f].wait()
        pl.when(has_next)(far[f].wait_send)
        for copy in (to_up[f], to_down[f]):
            copy.wait_send()
        for copy in (hop_up[f], hop_down[f]):
            pl.when(has_prev)(copy.wait_send)


def shards(slabs, tiles, coarse, up_weight, up_bias, gain_one, conv_one, bias_one, gain_two, conv_two, bias_two):
    deep, frames, lines, half = coarse.shape
    chans = up_weight.shape[2]
    rows, cols = 2 * lines, 2 * half
    native = coarse.transpose(1, 2, 3, 0).reshape(frames, lines * half, deep)
    row = lambda vec: vec.reshape(1, chans)
    vmem = pl.BlockSpec(memory_space=pltpu.VMEM)
    far_away = pl.BlockSpec(memory_space=pl.ANY)
    return pl.pallas_call(
        functools.partial(body, slabs, tiles),
        out_shape=jax.ShapeDtypeStruct((chans, frames, rows, cols), BF16),
        in_specs=[far_away] * 4 + [vmem] * 5,
        out_specs=far_away,
        scratch_shapes=[
            pltpu.VMEM((frames, lines * half, deep), BF16),
            pltpu.VMEM((2 * frames, 4, deep, cols), BF16),
            pltpu.VMEM((2 * chans, 4 * deep), BF16),
            pltpu.VMEM((2 * chans, 4 * deep), BF16),
            pltpu.VMEM((3 * chans, 9 * chans), BF16),
            pltpu.VMEM((3 * chans, 9 * chans), BF16),
            pltpu.VMEM((5, chans, cols), F32),
            pltpu.VMEM((2 * cols, 2 * cols), BF16),
            pltpu.VMEM((2 * frames, rows + 4, chans, cols), BF16),
            pltpu.VMEM((2 * frames, rows + 4, 3 * chans, cols), BF16),
            pltpu.VMEM((frames + 2, rows + 2, chans, cols), F32),
            pltpu.VMEM((frames + 2, rows + 2, 3 * chans, cols), BF16),
            pltpu.VMEM((frames, rows, chans, cols), F32),
            pltpu.VMEM(up_weight.shape, BF16),
            pltpu.VMEM(conv_one.shape, BF16),
            pltpu.VMEM(conv_two.shape, BF16),
            pltpu.VMEM((2, chans * rows, cols), F32),
            pltpu.VMEM((frames, chans, rows, cols), BF16),
            pltpu.SemaphoreType.DMA((frames,)),
            pltpu.SemaphoreType.DMA((3,)),
            pltpu.SemaphoreType.DMA((frames,)),
            pltpu.SemaphoreType.DMA((frames, 2)),
            pltpu.SemaphoreType.DMA((frames, 2)),
            pltpu.SemaphoreType.DMA((frames,)),
            pltpu.SemaphoreType.DMA((frames,)),
            pltpu.SemaphoreType.DMA((frames, 2)),
            pltpu.SemaphoreType.DMA((frames, 2)),
        ],
        compiler_params=pltpu.CompilerParams(collective_id=0, has_side_effects=True, vmem_limit_bytes=60 * 2**20),
    )(native, up_weight, conv_one, conv_two, row(up_bias), row(gain_one), row(bias_one), row(gain_two), row(bias_two))


def solution(mesh):
    return jax.shard_map(
        functools.partial(shards, mesh.shape["slab"], mesh.shape["tile"]),
        mesh=mesh,
        in_specs=(P(None, "slab", "tile", None), P(), P(), P(), P(), P(), P(), P(), P()),
        out_specs=P(None, "slab", "tile", None),
        check_vma=False,
    )
```

```python
import functools

import jax
import jax.numpy as jnp
from jax import lax
from jax.experimental import pallas as pl
from jax.experimental.pallas import tpu as pltpu
from jax.sharding import PartitionSpec as P

MESH = pl.DeviceIdType.MESH
F32 = jnp.float32
BF16 = jnp.bfloat16


def body(slabs, tiles, coarse, up_w, one_w, two_w, up_b, one_g, one_b, two_g, two_b, out,
         native, cbuf, we, wo, w1, g1, sums, g2, vecs, merge, vals, x1, acc1, x2, acc2, raw_u, raw_1, raw_2, spread, staged, fetch, load, leave,
         near_send, near_recv, far_send, far_recv, hop_send, hop_recv):
    frames = coarse.shape[0]
    chans, _, rows, _ = out.shape
    cols = cbuf.shape[3]
    half = cols // 2
    s = lax.axis_index("slab")
    t = lax.axis_index("tile")
    up, down = lax.rem(t + tiles - 1, tiles), lax.rem(t + 1, tiles)
    has_prev, has_next = s > 0, s < slabs - 1
    odd = lax.rem(t, 2)
    mate = t + 1 - 2 * odd
    wide_far = frames // 2

    def remote(src, dst, send, recv, who):
        return pltpu.make_async_remote_copy(
            src_ref=src, dst_ref=dst, send_sem=send, recv_sem=recv, device_id=who, device_id_type=MESH)

    fetches = [pltpu.make_async_copy(coarse.at[f], native.at[f], fetch.at[f]) for f in range(frames)]
    for copy in reversed(fetches):
        copy.start()

    barrier = pltpu.get_barrier_semaphore()
    for who in ({"tile": up}, {"tile": down}):
        pl.semaphore_signal(barrier, inc=1, device_id=who, device_id_type=MESH)
    for there, who in ((has_next, s + 1), (has_prev, s - 1)):
        @pl.when(there)
        def _():
            pl.semaphore_signal(barrier, inc=1, device_id={"slab": who}, device_id_type=MESH)

    loads = [pltpu.make_async_copy(src, dst, load.at[n])
             for n, (src, dst) in enumerate(((up_w, raw_u), (one_w, raw_1), (two_w, raw_2)))]
    for copy in loads:
        copy.start()

    to_up = [remote(cbuf.at[frames + f, 1], cbuf.at[frames + f, 3], near_send.at[f, 0], near_recv.at[f, 0], {"tile": up}) for f in range(frames)]
    to_down = [remote(cbuf.at[frames + f, 2], cbuf.at[frames + f, 0], near_send.at[f, 1], near_recv.at[f, 1], {"tile": down}) for f in range(frames)]
    spans = [pl.ds(odd, 3) if f < wide_far else pl.ds(1, 2) for f in range(frames)]
    far = [remote(cbuf.at[frames + f, spans[f]], cbuf.at[f, spans[f]], far_send.at[f], far_recv.at[f], {"slab": s + 1}) for f in range(frames)]
    hop_mate = [remote(cbuf.at[f, 2 - odd], cbuf.at[f, 3 * odd], hop_send.at[f, 0], hop_recv.at[f, 0], {"tile": mate}) for f in range(wide_far)]
    hop_up = [remote(cbuf.at[f, 1], cbuf.at[f, 3], hop_send.at[f, 0], hop_recv.at[f, 0], {"tile": up}) for f in range(frames)]
    hop_down = [remote(cbuf.at[f, 2], cbuf.at[f, 0], hop_send.at[f, 1], hop_recv.at[f, 1], {"tile": down}) for f in range(frames)]

    line = lax.broadcasted_iota(jnp.int32, (2 * cols, 2 * cols), 0)
    col = lax.broadcasted_iota(jnp.int32, (2 * cols, 2 * cols), 1)
    inner = jnp.bitwise_and(col, cols - 1)
    place = jnp.bitwise_and(col, cols) + lax.shift_right_arithmetic(inner, 1) + half * jnp.bitwise_and(inner, 1)
    merge[...] = jnp.where(line == place, 1.0, 0.0).astype(BF16)

    for n, vec in enumerate((up_b, one_g, one_b, two_g, two_b)):
        vecs[n] = jnp.transpose(jnp.broadcast_to(vec[...], (cols, chans)))

    for f in reversed(range(frames)):
        fetches[f].wait()
        turned = jnp.transpose(native[f])
        cbuf[frames + f, 1] = turned[:, :cols]
        cbuf[frames + f, 2] = turned[:, cols:]

    @pl.when(jnp.logical_not(has_prev))
    def _():
        for f in range(frames):
            for q in range(4):
                cbuf[f, q] = jnp.zeros(cbuf.shape[2:], BF16)

    pl.semaphore_wait(barrier, 2 + has_prev.astype(jnp.int32) + has_next.astype(jnp.int32))
    for f in reversed(range(frames)):
        to_up[f].start()
        to_down[f].start()

    def far_go(*sent):
        @pl.when(has_next)
        def _():
            for f in sent:
                far[f].start()

    far_go(*reversed(range(wide_far, frames)))

    loads[0].wait()
    for phase in range(2):
        lines = []
        for near_row in range(2):
            picks = ((0, 1), (2,)) if phase == 0 else ((0,), (1, 2))
            taps = picks[near_row]
            lines.append([sum(raw_u[a, b].astype(F32) for a in taps) for b in range(3)])
        for w, pick in ((we, lambda u: (u[0], u[1] + u[2])), (wo, lambda u: (u[0] + u[1], u[2]))):
            w[phase * chans:(phase + 1) * chans] = jnp.concatenate(
                [piece for u in lines for piece in pick(u)], axis=1).astype(BF16)
    full = g1.shape[2] - chans
    for n, raw, ends, mids_of in ((1, raw_1, g1, 0), (2, raw_2, g2, 2)):
        loads[n].wait()
        for tap in range(3):
            place = pl.ds(tap * chans, chans)
            taps = [raw[tap, a] for a in range(3)]
            if n == 1:
                w1[place] = jnp.concatenate(taps, axis=1)
            whole = [w[:, :full].astype(F32) for w in taps]
            side = jnp.concatenate([w[:, full:] for w in taps], axis=1)
            ends[0, place] = jnp.concatenate([taps[0][:, :full], side], axis=1)
            ends[1, place] = jnp.concatenate([-taps[2][:, :full], side], axis=1)
            outer_two = 0.5 * (whole[0] + whole[2])
            sums[mids_of, place] = (outer_two + 0.5 * whole[1]).astype(BF16)
            sums[mids_of + 1, place] = (outer_two - 0.5 * whole[1]).astype(BF16)

    def lanes_of(depth):
        return lax.broadcasted_iota(jnp.int32, (depth, cols), 1)

    deep = cbuf.shape[2]
    low_deep = lanes_of(deep) < half
    open_left = jnp.bitwise_and(lanes_of(deep), half - 1) != 0
    open_right = jnp.bitwise_and(lanes_of(deep), half - 1) != half - 1
    low = lanes_of(chans) < half
    first = lanes_of(chans) == 0
    last = lanes_of(chans) == cols - 1
    none_deep = jnp.zeros((deep, cols), BF16)
    none = jnp.zeros((chans, cols), BF16)

    def norm_act(values, gain, keep):
        meansq = jnp.mean(values * values, axis=0, keepdims=True)
        y = values * (lax.rsqrt(meansq + 1e-06) * (0.5 * keep)) * gain
        return y + y * jnp.tanh(y)

    def put(ref, f, r, act):
        mid = act.astype(BF16)
        cross = pltpu.roll(mid, half, 1)
        left = jnp.where(first, none, jnp.where(low, pltpu.roll(mid, half + 1, 1), cross))
        right = jnp.where(last, none, jnp.where(low, cross, pltpu.roll(mid, half - 1, 1)))

        def store():
            for b, piece in enumerate((left, mid, right)):
                ref[f, r, pl.ds(b * chans, chans)] = piece
        return store

    def run(trips, *steps):
        for i in range(trips):
            for store in [store for step in steps for store in step(i)]:
                store()

    top_keep = jnp.where(t > 0, 1.0, 0.0)
    bottom_keep = jnp.where(t < tiles - 1, 1.0, 0.0)
    past_keep = jnp.where(s > 0, 1.0, 0.0)
    top_mask = jnp.full((deep, cols), top_keep, F32).astype(BF16)
    bottom_mask = jnp.full((deep, cols), bottom_keep, F32).astype(BF16)

    def row_keep(r, lo, hi):
        return top_keep if r < lo else bottom_keep if r >= hi else 1.0

    def windows(f, kind):
        def lines(q):
            got = cbuf[f, q]
            return got * top_mask if q == 0 else got * bottom_mask if q == 3 else got

        def between(q):
            one, two = lines(q), lines(q + 1)
            return (jnp.where(low_deep, pltpu.roll(one, half, 1), pltpu.roll(two, half, 1)),
                    jnp.where(low_deep, two, one))
        if kind < 2:
            here, (below, below_swap) = lines(kind), between(kind)
            swap = pltpu.roll(here, half, 1)
        elif kind == 2:
            here = below_swap = lines(2)
            swap = below = pltpu.roll(here, half, 1)
        else:
            (here, swap), below = between(2), lines(3)
            below_swap = pltpu.roll(below, half, 1)

        def to_left(v):
            return jnp.where(open_left, pltpu.roll(v, 1, 1), none_deep)

        def to_right(v):
            return jnp.where(open_right, pltpu.roll(v, cols - 1, 1), none_deep)
        even = jnp.concatenate([to_left(here), here, to_left(below), below], axis=0)
        odd = jnp.concatenate([swap, to_right(swap), below_swap, to_right(below_swap)], axis=0)
        return even, odd

    def grow(*jobs):
        cut = [windows(f, p) for f, p in jobs]
        even, odd = [jnp.dot(w[...], jnp.concatenate([c[k] for c in cut], axis=1), preferred_element_type=F32)
                     for k, w in enumerate((we, wo))]
        stores = []
        for k, (f, p) in enumerate(jobs):
            for phase in range(2):
                e = even[phase * chans:(phase + 1) * chans, k * cols:(k + 1) * cols] + vecs[0]
                o = odd[phase * chans:(phase + 1) * chans, k * cols:(k + 1) * cols] + vecs[0]
                for side in range(1 if p == 2 else 2):
                    r = 2 * ((0, 2, 4, 5)[p] + side) - 1 + phase
                    if 0 <= r < rows + 4:
                        if side == 0:
                            value = jnp.where(lanes_of(chans) < half, e, o).astype(BF16)
                        else:
                            value = pltpu.roll(jnp.where(lanes_of(chans) < half, o, e).astype(BF16), half, 1)

                        def store(f=f, r=r, value=value):
                            vals[f, r] = value
                        stores.append(store)
        return stores

    def growing(*works):
        return lambda i: grow(*works[i]) if i < len(works) else []

    def finish(f, r):
        keep = row_keep(r, 2, rows + 2)
        if f < frames:
            keep = keep * past_keep
        return put(x1, f, r, norm_act(vals[f, r].astype(F32), vecs[1], keep))

    inner = list(range(3, rows + 1))
    outer = [r for r in range(rows + 4) if r not in inner]

    def finishing(f, lines, trips):
        each = -(-len(lines) // trips)
        return lambda i: [finish(f, r) for r in lines[i * each:(i + 1) * each]]

    def conv(x, w, ends, mids_of, acc, f, newest_out, works, start_of, done):
        taps = [tap for tap in range(3) if 0 <= f - tap <= newest_out]
        lo, hi = taps[0], taps[-1] + 1
        part = pl.ds(lo * chans, (hi - lo) * chans)

        def dot(weights, rhs):
            return jnp.dot(weights, rhs, preferred_element_type=F32)

        def apart(pair):
            rhs = jnp.concatenate(
                [jnp.concatenate([x[f, r + a] for r in pair], axis=1) for a in range(3)], axis=0)
            got = dot(w[part], rhs)
            return [(r, got, j) for j, r in enumerate(pair)]

        def fours(*firsts):
            d = [jnp.concatenate([x[f, r + a, :full] for r in firsts], axis=1) for a in range(4)]
            e = [jnp.concatenate([x[f, r + a, full:] for r in firsts], axis=1) for a in range(4)]
            plus = dot(sums[mids_of, part], d[1] + d[2])
            minus = dot(sums[mids_of + 1, part], d[2] - d[1])
            even = dot(ends[0, part], jnp.concatenate([d[0] - d[2], e[0], e[1], e[2]], axis=0)) + (plus + minus)
            odd_row = dot(ends[1, part], jnp.concatenate([d[1] - d[3], e[1], e[2], e[3]], axis=0)) + (plus - minus)
            return [(r + k, got, j) for j, r in enumerate(firsts) for k, got in enumerate((even, odd_row))]

        def step(p):
            if p >= len(works):
                return []
            kind, rows_of = works[p]
            results = apart(rows_of) if kind == 0 else fours(*rows_of)

            def store():
                for tap in taps:
                    n = f - tap
                    totals = []
                    for r, got, j in results:
                        mine = got[(tap - lo) * chans:(tap - lo + 1) * chans, j * cols:(j + 1) * cols]
                        totals.append((r, mine + (start_of(n, r) if tap == 2 else acc[n, r])))
                    if tap == 0 and done is not None:
                        for k in range(0, len(totals), 2):
                            done(n, [r for r, _ in totals[k:k + 2]], [total for _, total in totals[k:k + 2]])
                    else:
                        for r, total in totals:
                            acc[n, r] = total
            return [store]
        return step

    mids = frames + 2

    early = [(1, (r, r + 2)) for r in range(3, rows - 1, 4)]
    late = [(1, (1, rows - 1)), (0, (0, rows + 1))]

    def conv_a(f, pairs=early + late):
        return conv(x1, w1, g1, 0, acc1, f, mids - 1, pairs, lambda n, r: vecs[2], None)

    def finished(n, pair, totals):
        flat = jnp.concatenate([total.astype(BF16) for total in totals], axis=1)
        wide = jnp.dot(flat, merge[...], preferred_element_type=F32)
        for j, r in enumerate(pair):
            spread[n % 2, pl.ds(r, chans, stride=rows)] = wide[:, j * cols:(j + 1) * cols]

    leaving = [pltpu.make_async_copy(staged.at[n], out.at[:, n], leave.at[n]) for n in range(frames)]

    def emit(n):
        staged[n] = spread[n % 2].reshape(chans, rows, cols).astype(BF16)
        leaving[n].start()

    def conv_b(f):
        return conv(x2, None, g2, 2, acc2, f, frames - 1, [(1, (r, r + 2)) for r in range(0, rows, 4)], lambda n, r: vals[frames + n, r + 2].astype(F32) + vecs[4], finished)

    def second(n, r):
        keep = row_keep(r, 1, rows + 1)
        if n < 2:
            keep = keep * past_keep
        return put(x2, n, r, norm_act(acc1[n, r], vecs[3], keep))

    def second_two(n):
        return lambda p: [second(n, 2 * p), second(n, 2 * p + 1)] if 2 * p < rows + 2 else []

    def arrived(f):
        to_up[f - frames].wait_recv()
        to_down[f - frames].wait_recv()

    def hops(f):
        return [hop_mate[f]] if f < wide_far else [hop_up[f], hop_down[f]]

    def relay(*sent):
        for f in sent:
            far[f].wait_recv()
            for copy in hops(f):
                copy.start()

    def landed(*sent):
        for f in sent:
            for copy in hops(f):
                copy.wait_recv()

    def middle(f):
        return growing(((f, 1), (f, 2)))

    def rim(f):
        return growing(((f, 0), (f, 3)))

    wide_pairs = (rows + 2) // 2
    lines = list(range(rows + 4))
    n = 2 * frames
    run(1, middle(n - 1))
    run(1, middle(n - 2), finishing(n - 1, inner, 1))
    run(2, middle(n - 3), conv_a(n - 1, early), finishing(n - 2, inner, 2))
    run(2, middle(n - 4), conv_a(n - 2, early), finishing(n - 3, inner, 2))
    run(2, conv_a(n - 3, early), finishing(n - 4, inner, 2))
    run(2, conv_a(n - 4, early))
    def rims(f, *others):
        run(1, rim(f), *others)

    arrived(n - 1)
    arrived(n - 2)
    rims(n - 1)
    rims(n - 2, finishing(n - 1, outer, 1))
    run(3, conv_a(n - 1, late), finishing(n - 2, outer, 3))
    arrived(n - 3)
    arrived(n - 4)
    far_go(1, 0)
    rims(n - 3)
    run(3, conv_a(n - 2, late), finishing(n - 3, outer, 3), rim(n - 4))
    run(3, conv_a(n - 3, late), finishing(n - 4, outer, 3))
    pl.when(has_prev)(lambda: relay(3, 2))
    run(wide_pairs, conv_a(n - 4, late), second_two(5), middle(3))
    run(wide_pairs, second_two(4), conv_b(5), finishing(3, inner, 2), middle(2))
    run(4, conv_b(4), conv_a(3, early), finishing(2, inner, 3))
    run(3, conv_a(2, early))

    @pl.when(has_prev)
    def _():
        landed(3, 2)
        relay(1)
    run(2, rim(3), middle(1))
    run(3, rim(2), finishing(3, outer, 3))
    run(3, conv_a(3, late), finishing(2, outer, 3))
    run(wide_pairs, conv_a(2, late), second_two(3), finishing(1, inner, 3))

    @pl.when(has_prev)
    def _():
        relay(0)
        landed(1)
    run(wide_pairs, conv_b(3), second_two(2), middle(0))
    run(4, conv_b(2), conv_a(1, early), finishing(0, inner, 4), rim(1))
    emit(3)
    run(3, conv_a(0, early), finishing(1, outer, 1))
    emit(2)
    pl.when(has_prev)(lambda: landed(0))
    run(1, rim(0))
    run(3, conv_a(1, late), finishing(0, outer, 3))
    run(wide_pairs, conv_a(0, late), second_two(1))
    run(wide_pairs, conv_b(1), second_two(0))
    emit(1)
    run(4, conv_b(0))
    emit(0)

    for f in range(frames):
        leaving[f].wait()
        pl.when(has_next)(far[f].wait_send)
        for copy in (to_up[f], to_down[f]):
            copy.wait_send()
        for copy in hops(f):
            pl.when(has_prev)(copy.wait_send)


def shards(slabs, tiles, coarse, up_weight, up_bias, gain_one, conv_one, bias_one, gain_two, conv_two, bias_two):
    deep, frames, lines, half = coarse.shape
    chans = up_weight.shape[2]
    rows, cols = 2 * lines, 2 * half
    native = coarse.transpose(1, 2, 3, 0).reshape(frames, lines * half, deep)
    row = lambda vec: vec.reshape(1, chans)
    vmem = pl.BlockSpec(memory_space=pltpu.VMEM)
    far_away = pl.BlockSpec(memory_space=pl.ANY)
    return pl.pallas_call(
        functools.partial(body, slabs, tiles),
        out_shape=jax.ShapeDtypeStruct((chans, frames, rows, cols), BF16),
        in_specs=[far_away] * 4 + [vmem] * 5,
        out_specs=far_away,
        scratch_shapes=[
            pltpu.VMEM((frames, lines * half, deep), BF16),
            pltpu.VMEM((2 * frames, 4, deep, cols), BF16),
            pltpu.VMEM((2 * chans, 4 * deep), BF16),
            pltpu.VMEM((2 * chans, 4 * deep), BF16),
            pltpu.VMEM((3 * chans, 9 * chans), BF16),
            pltpu.VMEM((2, 3 * chans, 3 * chans // 256 * 256 + chans), BF16),
            pltpu.VMEM((4, 3 * chans, 3 * chans // 256 * 256), BF16),
            pltpu.VMEM((2, 3 * chans, 3 * chans // 256 * 256 + chans), BF16),
            pltpu.VMEM((5, chans, cols), F32),
            pltpu.VMEM((2 * cols, 2 * cols), BF16),
            pltpu.VMEM((2 * frames, rows + 4, chans, cols), BF16),
            pltpu.VMEM((2 * frames, rows + 4, 3 * chans, cols), BF16),
            pltpu.VMEM((frames + 2, rows + 2, chans, cols), F32),
            pltpu.VMEM((frames + 2, rows + 2, 3 * chans, cols), BF16),
            pltpu.VMEM((frames, rows, chans, cols), F32),
            pltpu.VMEM(up_weight.shape, BF16),
            pltpu.VMEM(conv_one.shape, BF16),
            pltpu.VMEM(conv_two.shape, BF16),
            pltpu.VMEM((2, chans * rows, cols), F32),
            pltpu.VMEM((frames, chans, rows, cols), BF16),
            pltpu.SemaphoreType.DMA((frames,)),
            pltpu.SemaphoreType.DMA((3,)),
            pltpu.SemaphoreType.DMA((frames,)),
            pltpu.SemaphoreType.DMA((frames, 2)),
            pltpu.SemaphoreType.DMA((frames, 2)),
            pltpu.SemaphoreType.DMA((frames,)),
            pltpu.SemaphoreType.DMA((frames,)),
            pltpu.SemaphoreType.DMA((frames, 2)),
            pltpu.SemaphoreType.DMA((frames, 2)),
        ],
        compiler_params=pltpu.CompilerParams(collective_id=0, has_side_effects=True, vmem_limit_bytes=60 * 2**20),
    )(native, up_weight, conv_one, conv_two, row(up_bias), row(gain_one), row(bias_one), row(gain_two), row(bias_two))


def solution(mesh):
    return jax.shard_map(
        functools.partial(shards, mesh.shape["slab"], mesh.shape["tile"]),
        mesh=mesh,
        in_specs=(P(None, "slab", "tile", None), P(), P(), P(), P(), P(), P(), P(), P()),
        out_specs=P(None, "slab", "tile", None),
        check_vma=False,
    )
```

```python
import functools

import jax
import jax.numpy as jnp
from jax import lax
from jax.experimental import pallas as pl
from jax.experimental.pallas import tpu as pltpu
from jax.sharding import PartitionSpec as P

MESH = pl.DeviceIdType.MESH
F32 = jnp.float32
BF16 = jnp.bfloat16


def body(slabs, tiles, coarse, up_w, one_w, two_w, up_b, one_g, one_b, two_g, two_b, out,
         native, cbuf, we, wo, w1, g1, sums, g2, vecs, merge, vals, x1, acc1, x2, acc2, raw_u, raw_1, raw_2, spread, staged, fetch, load, leave,
         near_send, near_recv, far_send, far_recv, hop_send, hop_recv):
    frames = coarse.shape[0]
    chans, _, rows, _ = out.shape
    cols = cbuf.shape[3]
    half = cols // 2
    s = lax.axis_index("slab")
    t = lax.axis_index("tile")
    up, down = lax.rem(t + tiles - 1, tiles), lax.rem(t + 1, tiles)
    has_prev, has_next = s > 0, s < slabs - 1
    odd = lax.rem(t, 2)
    mate = t + 1 - 2 * odd
    wide_far = frames // 2

    def remote(src, dst, send, recv, who):
        return pltpu.make_async_remote_copy(
            src_ref=src, dst_ref=dst, send_sem=send, recv_sem=recv, device_id=who, device_id_type=MESH)

    fetches = [pltpu.make_async_copy(coarse.at[f], native.at[f], fetch.at[f]) for f in range(frames)]
    for copy in reversed(fetches):
        copy.start()

    barrier = pltpu.get_barrier_semaphore()
    for who in ({"tile": up}, {"tile": down}):
        pl.semaphore_signal(barrier, inc=1, device_id=who, device_id_type=MESH)
    for there, who in ((has_next, s + 1), (has_prev, s - 1)):
        @pl.when(there)
        def _():
            pl.semaphore_signal(barrier, inc=1, device_id={"slab": who}, device_id_type=MESH)

    loads = [pltpu.make_async_copy(src, dst, load.at[n])
             for n, (src, dst) in enumerate(((up_w, raw_u), (one_w, raw_1), (two_w, raw_2)))]
    for copy in loads:
        copy.start()

    to_up = [remote(cbuf.at[frames + f, 1], cbuf.at[frames + f, 3], near_send.at[f, 0], near_recv.at[f, 0], {"tile": up}) for f in range(frames)]
    to_down = [remote(cbuf.at[frames + f, 2], cbuf.at[frames + f, 0], near_send.at[f, 1], near_recv.at[f, 1], {"tile": down}) for f in range(frames)]
    spans = [pl.ds(odd, 3) if f < wide_far else pl.ds(1, 2) for f in range(frames)]
    far = [remote(cbuf.at[frames + f, spans[f]], cbuf.at[f, spans[f]], far_send.at[f], far_recv.at[f], {"slab": s + 1}) for f in range(frames)]
    hop_mate = [remote(cbuf.at[f, 2 - odd], cbuf.at[f, 3 * odd], hop_send.at[f, 0], hop_recv.at[f, 0], {"tile": mate}) for f in range(wide_far)]
    hop_up = [remote(cbuf.at[f, 1], cbuf.at[f, 3], hop_send.at[f, 0], hop_recv.at[f, 0], {"tile": up}) for f in range(frames)]
    hop_down = [remote(cbuf.at[f, 2], cbuf.at[f, 0], hop_send.at[f, 1], hop_recv.at[f, 1], {"tile": down}) for f in range(frames)]

    for f in reversed(range(frames)):
        fetches[f].wait()
        turned = jnp.transpose(native[f])
        cbuf[frames + f, 1] = turned[:, :cols]
        cbuf[frames + f, 2] = turned[:, cols:]

    @pl.when(jnp.logical_not(has_prev))
    def _():
        for f in range(frames):
            for q in range(4):
                cbuf[f, q] = jnp.zeros(cbuf.shape[2:], BF16)

    pl.semaphore_wait(barrier, 2 + has_prev.astype(jnp.int32) + has_next.astype(jnp.int32))
    for f in reversed(range(frames)):
        to_up[f].start()
        to_down[f].start()

    def far_go(*sent):
        @pl.when(has_next)
        def _():
            for f in sent:
                far[f].start()

    far_go(*reversed(range(wide_far, frames)))

    line = lax.broadcasted_iota(jnp.int32, (2 * cols, 2 * cols), 0)
    col = lax.broadcasted_iota(jnp.int32, (2 * cols, 2 * cols), 1)
    inner = jnp.bitwise_and(col, cols - 1)
    place = jnp.bitwise_and(col, cols) + lax.shift_right_arithmetic(inner, 1) + half * jnp.bitwise_and(inner, 1)
    merge[...] = jnp.where(line == place, 1.0, 0.0).astype(BF16)

    for n, vec in enumerate((up_b, one_g, one_b, two_g, two_b)):
        vecs[n] = jnp.transpose(jnp.broadcast_to(vec[...], (cols, chans)))

    loads[0].wait()
    for phase in range(2):
        lines = []
        for near_row in range(2):
            picks = ((0, 1), (2,)) if phase == 0 else ((0,), (1, 2))
            taps = picks[near_row]
            lines.append([sum(raw_u[a, b].astype(F32) for a in taps) for b in range(3)])
        for w, pick in ((we, lambda u: (u[0], u[1] + u[2])), (wo, lambda u: (u[0] + u[1], u[2]))):
            w[phase * chans:(phase + 1) * chans] = jnp.concatenate(
                [piece for u in lines for piece in pick(u)], axis=1).astype(BF16)
    full = g1.shape[2] - chans
    for n, raw, ends, mids_of in ((1, raw_1, g1, 0), (2, raw_2, g2, 2)):
        loads[n].wait()
        for tap in range(3):
            place = pl.ds(tap * chans, chans)
            taps = [raw[tap, a] for a in range(3)]
            if n == 1:
                w1[place] = jnp.concatenate(taps, axis=1)
            whole = [w[:, :full].astype(F32) for w in taps]
            side = jnp.concatenate([w[:, full:] for w in taps], axis=1)
            ends[0, place] = jnp.concatenate([taps[0][:, :full], side], axis=1)
            ends[1, place] = jnp.concatenate([-taps[2][:, :full], side], axis=1)
            outer_two = 0.5 * (whole[0] + whole[2])
            sums[mids_of, place] = (outer_two + 0.5 * whole[1]).astype(BF16)
            sums[mids_of + 1, place] = (outer_two - 0.5 * whole[1]).astype(BF16)

    def lanes_of(depth):
        return lax.broadcasted_iota(jnp.int32, (depth, cols), 1)

    deep = cbuf.shape[2]
    low_deep = lanes_of(deep) < half
    open_left = jnp.bitwise_and(lanes_of(deep), half - 1) != 0
    open_right = jnp.bitwise_and(lanes_of(deep), half - 1) != half - 1
    low = lanes_of(chans) < half
    first = lanes_of(chans) == 0
    last = lanes_of(chans) == cols - 1
    none_deep = jnp.zeros((deep, cols), BF16)
    none = jnp.zeros((chans, cols), BF16)

    def norm_act(values, gain, keep):
        meansq = jnp.mean(values * values, axis=0, keepdims=True)
        y = values * (lax.rsqrt(meansq + 1e-06) * (0.5 * keep)) * gain
        return y + y * jnp.tanh(y)

    def put(ref, f, r, act):
        mid = act.astype(BF16)
        cross = pltpu.roll(mid, half, 1)
        left = jnp.where(first, none, jnp.where(low, pltpu.roll(mid, half + 1, 1), cross))
        right = jnp.where(last, none, jnp.where(low, cross, pltpu.roll(mid, half - 1, 1)))

        def store():
            for b, piece in enumerate((left, mid, right)):
                ref[f, r, pl.ds(b * chans, chans)] = piece
        return store

    def run(trips, *steps):
        for i in range(trips):
            for store in [store for step in steps for store in step(i)]:
                store()

    top_keep = jnp.where(t > 0, 1.0, 0.0)
    bottom_keep = jnp.where(t < tiles - 1, 1.0, 0.0)
    past_keep = jnp.where(s > 0, 1.0, 0.0)
    top_mask = jnp.full((deep, cols), top_keep, F32).astype(BF16)
    bottom_mask = jnp.full((deep, cols), bottom_keep, F32).astype(BF16)

    def row_keep(r, lo, hi):
        return top_keep if r < lo else bottom_keep if r >= hi else 1.0

    def windows(f, kind):
        def lines(q):
            got = cbuf[f, q]
            return got * top_mask if q == 0 else got * bottom_mask if q == 3 else got

        def between(q):
            one, two = lines(q), lines(q + 1)
            return (jnp.where(low_deep, pltpu.roll(one, half, 1), pltpu.roll(two, half, 1)),
                    jnp.where(low_deep, two, one))
        if kind < 2:
            here, (below, below_swap) = lines(kind), between(kind)
            swap = pltpu.roll(here, half, 1)
        elif kind == 2:
            here = below_swap = lines(2)
            swap = below = pltpu.roll(here, half, 1)
        else:
            (here, swap), below = between(2), lines(3)
            below_swap = pltpu.roll(below, half, 1)

        def to_left(v):
            return jnp.where(open_left, pltpu.roll(v, 1, 1), none_deep)

        def to_right(v):
            return jnp.where(open_right, pltpu.roll(v, cols - 1, 1), none_deep)
        even = jnp.concatenate([to_left(here), here, to_left(below), below], axis=0)
        odd = jnp.concatenate([swap, to_right(swap), below_swap, to_right(below_swap)], axis=0)
        return even, odd

    def grow(*jobs):
        cut = [windows(f, p) for f, p in jobs]
        even, odd = [jnp.dot(w[...], jnp.concatenate([c[k] for c in cut], axis=1), preferred_element_type=F32)
                     for k, w in enumerate((we, wo))]
        stores = []
        for k, (f, p) in enumerate(jobs):
            for phase in range(2):
                e = even[phase * chans:(phase + 1) * chans, k * cols:(k + 1) * cols] + vecs[0]
                o = odd[phase * chans:(phase + 1) * chans, k * cols:(k + 1) * cols] + vecs[0]
                for side in range(1 if p == 2 else 2):
                    r = 2 * ((0, 2, 4, 5)[p] + side) - 1 + phase
                    if 0 <= r < rows + 4:
                        if side == 0:
                            value = jnp.where(lanes_of(chans) < half, e, o).astype(BF16)
                        else:
                            value = pltpu.roll(jnp.where(lanes_of(chans) < half, o, e).astype(BF16), half, 1)

                        def store(f=f, r=r, value=value):
                            vals[f, r] = value
                        stores.append(store)
        return stores

    def growing(*works):
        return lambda i: grow(*works[i]) if i < len(works) else []

    def finish(f, r):
        keep = row_keep(r, 2, rows + 2)
        if f < frames:
            keep = keep * past_keep
        return put(x1, f, r, norm_act(vals[f, r].astype(F32), vecs[1], keep))

    inner = list(range(3, rows + 1))
    outer = [r for r in range(rows + 4) if r not in inner]

    def finishing(f, lines, trips):
        each = -(-len(lines) // trips)
        return lambda i: [finish(f, r) for r in lines[i * each:(i + 1) * each]]

    def conv(x, w, ends, mids_of, acc, f, newest_out, works, start_of, done):
        taps = [tap for tap in range(3) if 0 <= f - tap <= newest_out]
        lo, hi = taps[0], taps[-1] + 1
        part = pl.ds(lo * chans, (hi - lo) * chans)

        def dot(weights, rhs):
            return jnp.dot(weights, rhs, preferred_element_type=F32)

        def apart(pair):
            rhs = jnp.concatenate(
                [jnp.concatenate([x[f, r + a] for r in pair], axis=1) for a in range(3)], axis=0)
            got = dot(w[part], rhs)
            return [(r, got, j) for j, r in enumerate(pair)]

        def fours(*firsts):
            d = [jnp.concatenate([x[f, r + a, :full] for r in firsts], axis=1) for a in range(4)]
            e = [jnp.concatenate([x[f, r + a, full:] for r in firsts], axis=1) for a in range(4)]
            plus = dot(sums[mids_of, part], d[1] + d[2])
            minus = dot(sums[mids_of + 1, part], d[2] - d[1])
            even = dot(ends[0, part], jnp.concatenate([d[0] - d[2], e[0], e[1], e[2]], axis=0)) + (plus + minus)
            odd_row = dot(ends[1, part], jnp.concatenate([d[1] - d[3], e[1], e[2], e[3]], axis=0)) + (plus - minus)
            return [(r + k, got, j) for j, r in enumerate(firsts) for k, got in enumerate((even, odd_row))]

        def step(p):
            if p >= len(works):
                return []
            kind, rows_of = works[p]
            results = apart(rows_of) if kind == 0 else fours(*rows_of)

            def store():
                for tap in taps:
                    n = f - tap
                    totals = []
                    for r, got, j in results:
                        mine = got[(tap - lo) * chans:(tap - lo + 1) * chans, j * cols:(j + 1) * cols]
                        totals.append((r, mine + (start_of(n, r) if tap == 2 else acc[n, r])))
                    if tap == 0 and done is not None:
                        for k in range(0, len(totals), 2):
                            done(n, [r for r, _ in totals[k:k + 2]], [total for _, total in totals[k:k + 2]])
                    else:
                        for r, total in totals:
                            acc[n, r] = total
            return [store]
        return step

    mids = frames + 2

    early = [(1, (r, r + 2)) for r in range(3, rows - 1, 4)]
    late = [(1, (1, rows - 1)), (0, (0, rows + 1))]

    def conv_a(f, pairs=early + late):
        return conv(x1, w1, g1, 0, acc1, f, mids - 1, pairs, lambda n, r: vecs[2], None)

    def finished(n, pair, totals):
        flat = jnp.concatenate([total.astype(BF16) for total in totals], axis=1)
        wide = jnp.dot(flat, merge[...], preferred_element_type=F32)
        for j, r in enumerate(pair):
            spread[n % 2, pl.ds(r, chans, stride=rows)] = wide[:, j * cols:(j + 1) * cols]

    leaving = [pltpu.make_async_copy(staged.at[n], out.at[:, n], leave.at[n]) for n in range(frames)]

    def emit(n):
        staged[n] = spread[n % 2].reshape(chans, rows, cols).astype(BF16)
        leaving[n].start()

    def conv_b(f):
        return conv(x2, None, g2, 2, acc2, f, frames - 1, [(1, (r, r + 2)) for r in range(0, rows, 4)], lambda n, r: vals[frames + n, r + 2].astype(F32) + vecs[4], finished)

    def second(n, r):
        keep = row_keep(r, 1, rows + 1)
        if n < 2:
            keep = keep * past_keep
        return put(x2, n, r, norm_act(acc1[n, r], vecs[3], keep))

    def second_two(n):
        return lambda p: [second(n, 2 * p), second(n, 2 * p + 1)] if 2 * p < rows + 2 else []

    def arrived(f):
        to_up[f - frames].wait_recv()
        to_down[f - frames].wait_recv()

    def hops(f):
        return [hop_mate[f]] if f < wide_far else [hop_up[f], hop_down[f]]

    def relay(*sent):
        for f in sent:
            far[f].wait_recv()
            for copy in hops(f):
                copy.start()

    def landed(*sent):
        for f in sent:
            for copy in hops(f):
                copy.wait_recv()

    def middle(f):
        return growing(((f, 1), (f, 2)))

    def rim(f):
        return growing(((f, 0), (f, 3)))

    wide_pairs = (rows + 2) // 2
    lines = list(range(rows + 4))
    n = 2 * frames
    run(1, middle(n - 1))
    run(1, middle(n - 2), finishing(n - 1, inner, 1))
    run(2, middle(n - 3), conv_a(n - 1, early), finishing(n - 2, inner, 2))
    run(2, middle(n - 4), conv_a(n - 2, early), finishing(n - 3, inner, 2))
    run(2, conv_a(n - 3, early), finishing(n - 4, inner, 2))
    run(2, conv_a(n - 4, early))
    def rims(f, *others):
        run(1, rim(f), *others)

    arrived(n - 1)
    arrived(n - 2)
    rims(n - 1)
    rims(n - 2, finishing(n - 1, outer, 1))
    run(3, conv_a(n - 1, late), finishing(n - 2, outer, 3))
    arrived(n - 3)
    arrived(n - 4)
    far_go(1, 0)
    pl.when(has_prev)(lambda: relay(3))
    rims(n - 3)
    run(3, conv_a(n - 2, late), finishing(n - 3, outer, 3), rim(n - 4))
    run(3, conv_a(n - 3, late), finishing(n - 4, outer, 3))
    pl.when(has_prev)(lambda: relay(2))
    run(wide_pairs, conv_a(n - 4, late), second_two(5), middle(3))
    run(wide_pairs, second_two(4), conv_b(5), finishing(3, inner, 2), middle(2))
    run(4, conv_b(4), conv_a(3, early), finishing(2, inner, 3))
    run(3, conv_a(2, early))

    @pl.when(has_prev)
    def _():
        landed(3)
        relay(1)
    run(2, rim(3), middle(1))
    run(3, finishing(3, outer, 3), finishing(1, inner, 3))
    run(3, conv_a(3, late), conv_a(1, early))
    run(wide_pairs, second_two(3))
    run(4, conv_b(3))

    @pl.when(has_prev)
    def _():
        relay(0)
        landed(2, 1)
    run(1, rim(2))
    emit(3)
    run(3, rim(1), finishing(2, outer, 3))
    run(3, conv_a(2, late), middle(0), finishing(1, outer, 3))
    run(wide_pairs, second_two(2), conv_a(1, late), finishing(0, inner, 3))
    run(4, conv_b(2), conv_a(0, early))
    emit(2)
    pl.when(has_prev)(lambda: landed(0))
    run(1, rim(0))
    run(wide_pairs, finishing(0, outer, 3), second_two(1))
    run(wide_pairs, conv_a(0, late))
    run(wide_pairs, conv_b(1), second_two(0))
    emit(1)
    run(4, conv_b(0))
    emit(0)

    for f in range(frames):
        leaving[f].wait()
        pl.when(has_next)(far[f].wait_send)
        for copy in (to_up[f], to_down[f]):
            copy.wait_send()
        for copy in hops(f):
            pl.when(has_prev)(copy.wait_send)


def shards(slabs, tiles, coarse, up_weight, up_bias, gain_one, conv_one, bias_one, gain_two, conv_two, bias_two):
    deep, frames, lines, half = coarse.shape
    chans = up_weight.shape[2]
    rows, cols = 2 * lines, 2 * half
    native = coarse.transpose(1, 2, 3, 0).reshape(frames, lines * half, deep)
    row = lambda vec: vec.reshape(1, chans)
    vmem = pl.BlockSpec(memory_space=pltpu.VMEM)
    far_away = pl.BlockSpec(memory_space=pl.ANY)
    return pl.pallas_call(
        functools.partial(body, slabs, tiles),
        out_shape=jax.ShapeDtypeStruct((chans, frames, rows, cols), BF16),
        in_specs=[far_away] * 4 + [vmem] * 5,
        out_specs=far_away,
        scratch_shapes=[
            pltpu.VMEM((frames, lines * half, deep), BF16),
            pltpu.VMEM((2 * frames, 4, deep, cols), BF16),
            pltpu.VMEM((2 * chans, 4 * deep), BF16),
            pltpu.VMEM((2 * chans, 4 * deep), BF16),
            pltpu.VMEM((3 * chans, 9 * chans), BF16),
            pltpu.VMEM((2, 3 * chans, 3 * chans // 256 * 256 + chans), BF16),
            pltpu.VMEM((4, 3 * chans, 3 * chans // 256 * 256), BF16),
            pltpu.VMEM((2, 3 * chans, 3 * chans // 256 * 256 + chans), BF16),
            pltpu.VMEM((5, chans, cols), F32),
            pltpu.VMEM((2 * cols, 2 * cols), BF16),
            pltpu.VMEM((2 * frames, rows + 4, chans, cols), BF16),
            pltpu.VMEM((2 * frames, rows + 4, 3 * chans, cols), BF16),
            pltpu.VMEM((frames + 2, rows + 2, chans, cols), F32),
            pltpu.VMEM((frames + 2, rows + 2, 3 * chans, cols), BF16),
            pltpu.VMEM((frames, rows, chans, cols), F32),
            pltpu.VMEM(up_weight.shape, BF16),
            pltpu.VMEM(conv_one.shape, BF16),
            pltpu.VMEM(conv_two.shape, BF16),
            pltpu.VMEM((2, chans * rows, cols), F32),
            pltpu.VMEM((frames, chans, rows, cols), BF16),
            pltpu.SemaphoreType.DMA((frames,)),
            pltpu.SemaphoreType.DMA((3,)),
            pltpu.SemaphoreType.DMA((frames,)),
            pltpu.SemaphoreType.DMA((frames, 2)),
            pltpu.SemaphoreType.DMA((frames, 2)),
            pltpu.SemaphoreType.DMA((frames,)),
            pltpu.SemaphoreType.DMA((frames,)),
            pltpu.SemaphoreType.DMA((frames, 2)),
            pltpu.SemaphoreType.DMA((frames, 2)),
        ],
        compiler_params=pltpu.CompilerParams(collective_id=0, has_side_effects=True, vmem_limit_bytes=60 * 2**20),
    )(native, up_weight, conv_one, conv_two, row(up_bias), row(gain_one), row(bias_one), row(gain_two), row(bias_two))


def solution(mesh):
    return jax.shard_map(
        functools.partial(shards, mesh.shape["slab"], mesh.shape["tile"]),
        mesh=mesh,
        in_specs=(P(None, "slab", "tile", None), P(), P(), P(), P(), P(), P(), P(), P()),
        out_specs=P(None, "slab", "tile", None),
        check_vma=False,
    )
```

```python
import functools

import jax
import jax.numpy as jnp
from jax import lax
from jax.experimental import pallas as pl
from jax.experimental.pallas import tpu as pltpu
from jax.sharding import PartitionSpec as P

MESH = pl.DeviceIdType.MESH
F32 = jnp.float32
BF16 = jnp.bfloat16


def body(slabs, tiles, coarse, up_w, one_w, two_w, up_b, one_g, one_b, two_g, two_b, out,
         native, cbuf, we, wo, w1, g1, sums, g2, vecs, merge, vals, x1, acc1, x2, acc2, raw_u, raw_1, raw_2, spread, staged, fetch, load, leave,
         near_send, near_recv, far_send, far_recv, hop_send, hop_recv):
    frames = coarse.shape[0]
    chans, _, rows, _ = out.shape
    cols = cbuf.shape[3]
    half = cols // 2
    s = lax.axis_index("slab")
    t = lax.axis_index("tile")
    up, down = lax.rem(t + tiles - 1, tiles), lax.rem(t + 1, tiles)
    has_prev, has_next = s > 0, s < slabs - 1
    odd = lax.rem(t, 2)
    mate = t + 1 - 2 * odd
    wide_far = 1

    def remote(src, dst, send, recv, who):
        return pltpu.make_async_remote_copy(
            src_ref=src, dst_ref=dst, send_sem=send, recv_sem=recv, device_id=who, device_id_type=MESH)

    fetches = [pltpu.make_async_copy(coarse.at[f], native.at[f], fetch.at[f]) for f in range(frames)]
    for copy in reversed(fetches):
        copy.start()

    barrier = pltpu.get_barrier_semaphore()
    for who in ({"tile": up}, {"tile": down}):
        pl.semaphore_signal(barrier, inc=1, device_id=who, device_id_type=MESH)
    for there, who in ((has_next, s + 1), (has_prev, s - 1)):
        @pl.when(there)
        def _():
            pl.semaphore_signal(barrier, inc=1, device_id={"slab": who}, device_id_type=MESH)

    loads = [pltpu.make_async_copy(src, dst, load.at[n])
             for n, (src, dst) in enumerate(((up_w, raw_u), (one_w, raw_1), (two_w, raw_2)))]
    for copy in loads:
        copy.start()

    to_up = [remote(cbuf.at[frames + f, 1], cbuf.at[frames + f, 3], near_send.at[f, 0], near_recv.at[f, 0], {"tile": up}) for f in range(frames)]
    to_down = [remote(cbuf.at[frames + f, 2], cbuf.at[frames + f, 0], near_send.at[f, 1], near_recv.at[f, 1], {"tile": down}) for f in range(frames)]
    spans = [pl.ds(odd, 3) if f < wide_far else pl.ds(1, 2) for f in range(frames)]
    far = [remote(cbuf.at[frames + f, spans[f]], cbuf.at[f, spans[f]], far_send.at[f], far_recv.at[f], {"slab": s + 1}) for f in range(frames)]
    hop_mate = [remote(cbuf.at[f, 2 - odd], cbuf.at[f, 3 * odd], hop_send.at[f, 0], hop_recv.at[f, 0], {"tile": mate}) for f in range(wide_far)]
    hop_up = [remote(cbuf.at[f, 1], cbuf.at[f, 3], hop_send.at[f, 0], hop_recv.at[f, 0], {"tile": up}) for f in range(frames)]
    hop_down = [remote(cbuf.at[f, 2], cbuf.at[f, 0], hop_send.at[f, 1], hop_recv.at[f, 1], {"tile": down}) for f in range(frames)]

    for f in reversed(range(frames)):
        fetches[f].wait()
        turned = jnp.transpose(native[f])
        cbuf[frames + f, 1] = turned[:, :cols]
        cbuf[frames + f, 2] = turned[:, cols:]

    @pl.when(jnp.logical_not(has_prev))
    def _():
        for f in range(frames):
            for q in range(4):
                cbuf[f, q] = jnp.zeros(cbuf.shape[2:], BF16)

    pl.semaphore_wait(barrier, 2 + has_prev.astype(jnp.int32) + has_next.astype(jnp.int32))
    for f in reversed(range(frames)):
        to_up[f].start()
        to_down[f].start()

    def far_go(*sent):
        @pl.when(has_next)
        def _():
            for f in sent:
                far[f].start()

    far_go(*reversed(range(wide_far, frames)))

    line = lax.broadcasted_iota(jnp.int32, (2 * cols, 2 * cols), 0)
    col = lax.broadcasted_iota(jnp.int32, (2 * cols, 2 * cols), 1)
    inner = jnp.bitwise_and(col, cols - 1)
    place = jnp.bitwise_and(col, cols) + lax.shift_right_arithmetic(inner, 1) + half * jnp.bitwise_and(inner, 1)
    merge[...] = jnp.where(line == place, 1.0, 0.0).astype(BF16)

    for n, vec in enumerate((up_b, one_g, one_b, two_g, two_b)):
        vecs[n] = jnp.transpose(jnp.broadcast_to(vec[...], (cols, chans)))

    loads[0].wait()
    for phase in range(2):
        lines = []
        for near_row in range(2):
            picks = ((0, 1), (2,)) if phase == 0 else ((0,), (1, 2))
            taps = picks[near_row]
            lines.append([sum(raw_u[a, b].astype(F32) for a in taps) for b in range(3)])
        for w, pick in ((we, lambda u: (u[0], u[1] + u[2])), (wo, lambda u: (u[0] + u[1], u[2]))):
            w[phase * chans:(phase + 1) * chans] = jnp.concatenate(
                [piece for u in lines for piece in pick(u)], axis=1).astype(BF16)
    full = g1.shape[2] - chans
    for n, raw, ends, mids_of in ((1, raw_1, g1, 0), (2, raw_2, g2, 2)):
        loads[n].wait()
        for tap in range(3):
            place = pl.ds(tap * chans, chans)
            taps = [raw[tap, a] for a in range(3)]
            if n == 1:
                w1[place] = jnp.concatenate(taps, axis=1)
            whole = [w[:, :full].astype(F32) for w in taps]
            side = jnp.concatenate([w[:, full:] for w in taps], axis=1)
            ends[0, place] = jnp.concatenate([taps[0][:, :full], side], axis=1)
            ends[1, place] = jnp.concatenate([-taps[2][:, :full], side], axis=1)
            outer_two = 0.5 * (whole[0] + whole[2])
            sums[mids_of, place] = (outer_two + 0.5 * whole[1]).astype(BF16)
            sums[mids_of + 1, place] = (outer_two - 0.5 * whole[1]).astype(BF16)

    def lanes_of(depth):
        return lax.broadcasted_iota(jnp.int32, (depth, cols), 1)

    deep = cbuf.shape[2]
    low_deep = lanes_of(deep) < half
    open_left = jnp.bitwise_and(lanes_of(deep), half - 1) != 0
    open_right = jnp.bitwise_and(lanes_of(deep), half - 1) != half - 1
    low = lanes_of(chans) < half
    first = lanes_of(chans) == 0
    last = lanes_of(chans) == cols - 1
    none_deep = jnp.zeros((deep, cols), BF16)
    none = jnp.zeros((chans, cols), BF16)

    def norm_act(values, gain, keep):
        meansq = jnp.mean(values * values, axis=0, keepdims=True)
        y = values * (lax.rsqrt(meansq + 1e-06) * (0.5 * keep)) * gain
        return y + y * jnp.tanh(y)

    def put(ref, f, r, act):
        mid = act.astype(BF16)
        cross = pltpu.roll(mid, half, 1)
        left = jnp.where(first, none, jnp.where(low, pltpu.roll(mid, half + 1, 1), cross))
        right = jnp.where(last, none, jnp.where(low, cross, pltpu.roll(mid, half - 1, 1)))

        def store():
            for b, piece in enumerate((left, mid, right)):
                ref[f, r, pl.ds(b * chans, chans)] = piece
        return store

    def run(trips, *steps):
        for i in range(trips):
            for store in [store for step in steps for store in step(i)]:
                store()

    top_keep = jnp.where(t > 0, 1.0, 0.0)
    bottom_keep = jnp.where(t < tiles - 1, 1.0, 0.0)
    past_keep = jnp.where(s > 0, 1.0, 0.0)
    top_mask = jnp.full((deep, cols), top_keep, F32).astype(BF16)
    bottom_mask = jnp.full((deep, cols), bottom_keep, F32).astype(BF16)

    def row_keep(r, lo, hi):
        return top_keep if r < lo else bottom_keep if r >= hi else 1.0

    def windows(f, kind):
        def lines(q):
            got = cbuf[f, q]
            return got * top_mask if q == 0 else got * bottom_mask if q == 3 else got

        def between(q):
            one, two = lines(q), lines(q + 1)
            return (jnp.where(low_deep, pltpu.roll(one, half, 1), pltpu.roll(two, half, 1)),
                    jnp.where(low_deep, two, one))
        if kind < 2:
            here, (below, below_swap) = lines(kind), between(kind)
            swap = pltpu.roll(here, half, 1)
        elif kind == 2:
            here = below_swap = lines(2)
            swap = below = pltpu.roll(here, half, 1)
        else:
            (here, swap), below = between(2), lines(3)
            below_swap = pltpu.roll(below, half, 1)

        def to_left(v):
            return jnp.where(open_left, pltpu.roll(v, 1, 1), none_deep)

        def to_right(v):
            return jnp.where(open_right, pltpu.roll(v, cols - 1, 1), none_deep)
        even = jnp.concatenate([to_left(here), here, to_left(below), below], axis=0)
        odd = jnp.concatenate([swap, to_right(swap), below_swap, to_right(below_swap)], axis=0)
        return even, odd

    def grow(*jobs):
        cut = [windows(f, p) for f, p in jobs]
        even, odd = [jnp.dot(w[...], jnp.concatenate([c[k] for c in cut], axis=1), preferred_element_type=F32)
                     for k, w in enumerate((we, wo))]
        stores = []
        for k, (f, p) in enumerate(jobs):
            for phase in range(2):
                e = even[phase * chans:(phase + 1) * chans, k * cols:(k + 1) * cols] + vecs[0]
                o = odd[phase * chans:(phase + 1) * chans, k * cols:(k + 1) * cols] + vecs[0]
                for side in range(1 if p == 2 else 2):
                    r = 2 * ((0, 2, 4, 5)[p] + side) - 1 + phase
                    if 0 <= r < rows + 4:
                        if side == 0:
                            value = jnp.where(lanes_of(chans) < half, e, o).astype(BF16)
                        else:
                            value = pltpu.roll(jnp.where(lanes_of(chans) < half, o, e).astype(BF16), half, 1)

                        def store(f=f, r=r, value=value):
                            vals[f, r] = value
                        stores.append(store)
        return stores

    def growing(*works):
        return lambda i: grow(*works[i]) if i < len(works) else []

    def finish(f, r):
        keep = row_keep(r, 2, rows + 2)
        if f < frames:
            keep = keep * past_keep
        return put(x1, f, r, norm_act(vals[f, r].astype(F32), vecs[1], keep))

    inner = list(range(3, rows + 1))
    outer = [r for r in range(rows + 4) if r not in inner]

    def finishing(f, lines, trips):
        each = -(-len(lines) // trips)
        return lambda i: [finish(f, r) for r in lines[i * each:(i + 1) * each]]

    def conv(x, w, ends, mids_of, acc, f, newest_out, works, start_of, done):
        taps = [tap for tap in range(3) if 0 <= f - tap <= newest_out]
        lo, hi = taps[0], taps[-1] + 1
        part = pl.ds(lo * chans, (hi - lo) * chans)

        def dot(weights, rhs):
            return jnp.dot(weights, rhs, preferred_element_type=F32)

        def apart(pair):
            rhs = jnp.concatenate(
                [jnp.concatenate([x[f, r + a] for r in pair], axis=1) for a in range(3)], axis=0)
            got = dot(w[part], rhs)
            return [(r, got, j) for j, r in enumerate(pair)]

        def fours(*firsts):
            d = [jnp.concatenate([x[f, r + a, :full] for r in firsts], axis=1) for a in range(4)]
            e = [jnp.concatenate([x[f, r + a, full:] for r in firsts], axis=1) for a in range(4)]
            plus = dot(sums[mids_of, part], d[1] + d[2])
            minus = dot(sums[mids_of + 1, part], d[2] - d[1])
            even = dot(ends[0, part], jnp.concatenate([d[0] - d[2], e[0], e[1], e[2]], axis=0)) + (plus + minus)
            odd_row = dot(ends[1, part], jnp.concatenate([d[1] - d[3], e[1], e[2], e[3]], axis=0)) + (plus - minus)
            return [(r + k, got, j) for j, r in enumerate(firsts) for k, got in enumerate((even, odd_row))]

        def step(p):
            if p >= len(works):
                return []
            kind, rows_of = works[p]
            results = apart(rows_of) if kind == 0 else fours(*rows_of)

            def store():
                for tap in taps:
                    n = f - tap
                    totals = []
                    for r, got, j in results:
                        mine = got[(tap - lo) * chans:(tap - lo + 1) * chans, j * cols:(j + 1) * cols]
                        totals.append((r, mine + (start_of(n, r) if tap == 2 else acc[n, r])))
                    if tap == 0 and done is not None:
                        for k in range(0, len(totals), 2):
                            done(n, [r for r, _ in totals[k:k + 2]], [total for _, total in totals[k:k + 2]])
                    else:
                        for r, total in totals:
                            acc[n, r] = total
            return [store]
        return step

    mids = frames + 2

    early = [(1, (r, r + 2)) for r in range(3, rows - 1, 4)]
    late = [(1, (1, rows - 1)), (0, (0, rows + 1))]

    def conv_a(f, pairs=early + late):
        return conv(x1, w1, g1, 0, acc1, f, mids - 1, pairs, lambda n, r: vecs[2], None)

    def finished(n, pair, totals):
        flat = jnp.concatenate([total.astype(BF16) for total in totals], axis=1)
        wide = jnp.dot(flat, merge[...], preferred_element_type=F32)
        for j, r in enumerate(pair):
            spread[n % 2, pl.ds(r, chans, stride=rows)] = wide[:, j * cols:(j + 1) * cols]

    leaving = [pltpu.make_async_copy(staged.at[n], out.at[:, n], leave.at[n]) for n in range(frames)]

    def emit(n):
        staged[n] = spread[n % 2].reshape(chans, rows, cols).astype(BF16)
        leaving[n].start()

    def conv_b(f):
        return conv(x2, None, g2, 2, acc2, f, frames - 1, [(1, (r, r + 2)) for r in range(0, rows, 4)], lambda n, r: vals[frames + n, r + 2].astype(F32) + vecs[4], finished)

    def second(n, r):
        keep = row_keep(r, 1, rows + 1)
        if n < 2:
            keep = keep * past_keep
        return put(x2, n, r, norm_act(acc1[n, r], vecs[3], keep))

    def second_two(n):
        return lambda p: [second(n, 2 * p), second(n, 2 * p + 1)] if 2 * p < rows + 2 else []

    def arrived(f):
        to_up[f - frames].wait_recv()
        to_down[f - frames].wait_recv()

    def hops(f):
        return [hop_mate[f]] if f < wide_far else [hop_up[f], hop_down[f]]

    def relay(*sent):
        for f in sent:
            far[f].wait_recv()
            for copy in hops(f):
                copy.start()

    def landed(*sent):
        for f in sent:
            for copy in hops(f):
                copy.wait_recv()

    def middle(f):
        return growing(((f, 1), (f, 2)))

    def rim(f):
        return growing(((f, 0), (f, 3)))

    wide_pairs = (rows + 2) // 2
    lines = list(range(rows + 4))
    n = 2 * frames
    run(1, middle(n - 1))
    run(1, middle(n - 2), finishing(n - 1, inner, 1))
    run(2, middle(n - 3), conv_a(n - 1, early), finishing(n - 2, inner, 2))
    run(2, middle(n - 4), conv_a(n - 2, early), finishing(n - 3, inner, 2))
    run(2, conv_a(n - 3, early), finishing(n - 4, inner, 2))
    run(2, conv_a(n - 4, early))
    def rims(f, *others):
        run(1, rim(f), *others)

    arrived(n - 1)
    arrived(n - 2)
    rims(n - 1)
    rims(n - 2, finishing(n - 1, outer, 1))
    run(3, conv_a(n - 1, late), finishing(n - 2, outer, 3))
    arrived(n - 3)
    arrived(n - 4)
    far_go(0)
    pl.when(has_prev)(lambda: relay(3))
    rims(n - 3)
    run(3, conv_a(n - 2, late), finishing(n - 3, outer, 3), rim(n - 4))
    run(3, conv_a(n - 3, late), finishing(n - 4, outer, 3))
    pl.when(has_prev)(lambda: relay(2))
    run(wide_pairs, conv_a(n - 4, late), second_two(5), middle(3))
    run(wide_pairs, second_two(4), conv_b(5), finishing(3, inner, 2), middle(2))
    run(4, conv_b(4), conv_a(3, early), finishing(2, inner, 3))
    run(3, conv_a(2, early))

    @pl.when(has_prev)
    def _():
        landed(3)
        relay(1)
    run(2, rim(3), middle(1))
    run(3, finishing(3, outer, 3), finishing(1, inner, 3))
    run(3, conv_a(3, late), conv_a(1, early))
    run(wide_pairs, second_two(3))
    run(4, conv_b(3))

    @pl.when(has_prev)
    def _():
        relay(0)
        landed(2, 1)
    run(1, rim(2))
    emit(3)
    run(3, rim(1), finishing(2, outer, 3))
    run(3, conv_a(2, late), middle(0), finishing(1, outer, 3))
    run(wide_pairs, second_two(2), conv_a(1, late), finishing(0, inner, 3))
    run(4, conv_b(2), conv_a(0, early))
    emit(2)
    pl.when(has_prev)(lambda: landed(0))
    run(1, rim(0))
    run(wide_pairs, finishing(0, outer, 3), second_two(1))
    run(wide_pairs, conv_a(0, late))
    run(wide_pairs, conv_b(1), second_two(0))
    emit(1)
    run(4, conv_b(0))
    emit(0)

    for f in range(frames):
        leaving[f].wait()
        pl.when(has_next)(far[f].wait_send)
        for copy in (to_up[f], to_down[f]):
            copy.wait_send()
        for copy in hops(f):
            pl.when(has_prev)(copy.wait_send)


def shards(slabs, tiles, coarse, up_weight, up_bias, gain_one, conv_one, bias_one, gain_two, conv_two, bias_two):
    deep, frames, lines, half = coarse.shape
    chans = up_weight.shape[2]
    rows, cols = 2 * lines, 2 * half
    native = coarse.transpose(1, 2, 3, 0).reshape(frames, lines * half, deep)
    row = lambda vec: vec.reshape(1, chans)
    vmem = pl.BlockSpec(memory_space=pltpu.VMEM)
    far_away = pl.BlockSpec(memory_space=pl.ANY)
    return pl.pallas_call(
        functools.partial(body, slabs, tiles),
        out_shape=jax.ShapeDtypeStruct((chans, frames, rows, cols), BF16),
        in_specs=[far_away] * 4 + [vmem] * 5,
        out_specs=far_away,
        scratch_shapes=[
            pltpu.VMEM((frames, lines * half, deep), BF16),
            pltpu.VMEM((2 * frames, 4, deep, cols), BF16),
            pltpu.VMEM((2 * chans, 4 * deep), BF16),
            pltpu.VMEM((2 * chans, 4 * deep), BF16),
            pltpu.VMEM((3 * chans, 9 * chans), BF16),
            pltpu.VMEM((2, 3 * chans, 3 * chans // 256 * 256 + chans), BF16),
            pltpu.VMEM((4, 3 * chans, 3 * chans // 256 * 256), BF16),
            pltpu.VMEM((2, 3 * chans, 3 * chans // 256 * 256 + chans), BF16),
            pltpu.VMEM((5, chans, cols), F32),
            pltpu.VMEM((2 * cols, 2 * cols), BF16),
            pltpu.VMEM((2 * frames, rows + 4, chans, cols), BF16),
            pltpu.VMEM((2 * frames, rows + 4, 3 * chans, cols), BF16),
            pltpu.VMEM((frames + 2, rows + 2, chans, cols), F32),
            pltpu.VMEM((frames + 2, rows + 2, 3 * chans, cols), BF16),
            pltpu.VMEM((frames, rows, chans, cols), F32),
            pltpu.VMEM(up_weight.shape, BF16),
            pltpu.VMEM(conv_one.shape, BF16),
            pltpu.VMEM(conv_two.shape, BF16),
            pltpu.VMEM((2, chans * rows, cols), F32),
            pltpu.VMEM((frames, chans, rows, cols), BF16),
            pltpu.SemaphoreType.DMA((frames,)),
            pltpu.SemaphoreType.DMA((3,)),
            pltpu.SemaphoreType.DMA((frames,)),
            pltpu.SemaphoreType.DMA((frames, 2)),
            pltpu.SemaphoreType.DMA((frames, 2)),
            pltpu.SemaphoreType.DMA((frames,)),
            pltpu.SemaphoreType.DMA((frames,)),
            pltpu.SemaphoreType.DMA((frames, 2)),
            pltpu.SemaphoreType.DMA((frames, 2)),
        ],
        compiler_params=pltpu.CompilerParams(collective_id=0, has_side_effects=True, vmem_limit_bytes=60 * 2**20),
    )(native, up_weight, conv_one, conv_two, row(up_bias), row(gain_one), row(bias_one), row(gain_two), row(bias_two))


def solution(mesh):
    return jax.shard_map(
        functools.partial(shards, mesh.shape["slab"], mesh.shape["tile"]),
        mesh=mesh,
        in_specs=(P(None, "slab", "tile", None), P(), P(), P(), P(), P(), P(), P(), P()),
        out_specs=P(None, "slab", "tile", None),
        check_vma=False,
    )
```

```python
import functools

import jax
import jax.numpy as jnp
from jax import lax
from jax.experimental import pallas as pl
from jax.experimental.pallas import tpu as pltpu
from jax.sharding import PartitionSpec as P

MESH = pl.DeviceIdType.MESH
F32 = jnp.float32
BF16 = jnp.bfloat16


def body(slabs, tiles, coarse, up_w, one_w, two_w, up_b, one_g, one_b, two_g, two_b, out,
         native, cbuf, we, wo, w1, g1, sums, g2, vecs, merge, vals, x1, acc1, x2, acc2, raw_u, raw_1, raw_2, spread, staged, fetch, load, leave,
         near_send, near_recv, far_send, far_recv, hop_send, hop_recv):
    frames = coarse.shape[0]
    chans, _, rows, _ = out.shape
    cols = cbuf.shape[3]
    half = cols // 2
    s = lax.axis_index("slab")
    t = lax.axis_index("tile")
    up, down = lax.rem(t + tiles - 1, tiles), lax.rem(t + 1, tiles)
    has_prev, has_next = s > 0, s < slabs - 1
    odd = lax.rem(t, 2)
    mate = t + 1 - 2 * odd
    wide_far = 1

    def remote(src, dst, send, recv, who):
        return pltpu.make_async_remote_copy(
            src_ref=src, dst_ref=dst, send_sem=send, recv_sem=recv, device_id=who, device_id_type=MESH)

    fetches = [pltpu.make_async_copy(coarse.at[f], native.at[f], fetch.at[f]) for f in range(frames)]
    for copy in reversed(fetches):
        copy.start()

    barrier = pltpu.get_barrier_semaphore()
    for who in ({"tile": up}, {"tile": down}):
        pl.semaphore_signal(barrier, inc=1, device_id=who, device_id_type=MESH)
    for there, who in ((has_next, s + 1), (has_prev, s - 1)):
        @pl.when(there)
        def _():
            pl.semaphore_signal(barrier, inc=1, device_id={"slab": who}, device_id_type=MESH)

    loads = [pltpu.make_async_copy(src, dst, load.at[n])
             for n, (src, dst) in enumerate(((up_w, raw_u), (one_w, raw_1), (two_w, raw_2)))]
    for copy in loads:
        copy.start()

    cross = lax.rem(t + tiles - 1 + 2 * odd, tiles)
    to_cross = [remote(cbuf.at[frames + f, 1 + odd], cbuf.at[frames + f, 3 - 3 * odd], near_send.at[f, 0], near_recv.at[f, 0], {"tile": cross}) for f in range(frames)]
    to_mate = [remote(cbuf.at[frames + f, 2 - odd], cbuf.at[frames + f, 3 * odd], near_send.at[f, 1], near_recv.at[f, 1], {"tile": mate}) for f in range(frames)]
    spans = [pl.ds(odd, 3) if f < wide_far else pl.ds(1, 2) for f in range(frames)]
    far = [remote(cbuf.at[frames + f, spans[f]], cbuf.at[f, spans[f]], far_send.at[f], far_recv.at[f], {"slab": s + 1}) for f in range(frames)]
    hop_mate = [remote(cbuf.at[f, 2 - odd], cbuf.at[f, 3 * odd], hop_send.at[f, 0], hop_recv.at[f, 0], {"tile": mate}) for f in range(wide_far)]
    hop_up = [remote(cbuf.at[f, 1], cbuf.at[f, 3], hop_send.at[f, 0], hop_recv.at[f, 0], {"tile": up}) for f in range(frames)]
    hop_down = [remote(cbuf.at[f, 2], cbuf.at[f, 0], hop_send.at[f, 1], hop_recv.at[f, 1], {"tile": down}) for f in range(frames)]

    for f in reversed(range(frames)):
        fetches[f].wait()
        turned = jnp.transpose(native[f])
        cbuf[frames + f, 1] = turned[:, :cols]
        cbuf[frames + f, 2] = turned[:, cols:]

    @pl.when(jnp.logical_not(has_prev))
    def _():
        for f in range(frames):
            for q in range(4):
                cbuf[f, q] = jnp.zeros(cbuf.shape[2:], BF16)

    pl.semaphore_wait(barrier, 2 + has_prev.astype(jnp.int32) + has_next.astype(jnp.int32))
    for f in reversed(range(frames)):
        to_cross[f].start()
    for f in reversed(range(frames)):
        to_mate[f].start()

    def far_go(*sent):
        @pl.when(has_next)
        def _():
            for f in sent:
                far[f].start()

    far_go(*reversed(range(wide_far, frames)))

    line = lax.broadcasted_iota(jnp.int32, (2 * cols, 2 * cols), 0)
    col = lax.broadcasted_iota(jnp.int32, (2 * cols, 2 * cols), 1)
    inner = jnp.bitwise_and(col, cols - 1)
    place = jnp.bitwise_and(col, cols) + lax.shift_right_arithmetic(inner, 1) + half * jnp.bitwise_and(inner, 1)
    merge[...] = jnp.where(line == place, 1.0, 0.0).astype(BF16)

    for n, vec in enumerate((up_b, one_g, one_b, two_g, two_b)):
        vecs[n] = jnp.transpose(jnp.broadcast_to(vec[...], (cols, chans)))

    loads[0].wait()
    for phase in range(2):
        lines = []
        for near_row in range(2):
            picks = ((0, 1), (2,)) if phase == 0 else ((0,), (1, 2))
            taps = picks[near_row]
            lines.append([sum(raw_u[a, b].astype(F32) for a in taps) for b in range(3)])
        for w, pick in ((we, lambda u: (u[0], u[1] + u[2])), (wo, lambda u: (u[0] + u[1], u[2]))):
            w[phase * chans:(phase + 1) * chans] = jnp.concatenate(
                [piece for u in lines for piece in pick(u)], axis=1).astype(BF16)
    full = g1.shape[2] - chans
    for n, raw, ends, mids_of in ((1, raw_1, g1, 0), (2, raw_2, g2, 2)):
        loads[n].wait()
        for tap in range(3):
            place = pl.ds(tap * chans, chans)
            taps = [raw[tap, a] for a in range(3)]
            if n == 1:
                w1[place] = jnp.concatenate(taps, axis=1)
            whole = [w[:, :full].astype(F32) for w in taps]
            side = jnp.concatenate([w[:, full:] for w in taps], axis=1)
            ends[0, place] = jnp.concatenate([taps[0][:, :full], side], axis=1)
            ends[1, place] = jnp.concatenate([-taps[2][:, :full], side], axis=1)
            outer_two = 0.5 * (whole[0] + whole[2])
            sums[mids_of, place] = (outer_two + 0.5 * whole[1]).astype(BF16)
            sums[mids_of + 1, place] = (outer_two - 0.5 * whole[1]).astype(BF16)

    def lanes_of(depth):
        return lax.broadcasted_iota(jnp.int32, (depth, cols), 1)

    deep = cbuf.shape[2]
    low_deep = lanes_of(deep) < half
    open_left = jnp.bitwise_and(lanes_of(deep), half - 1) != 0
    open_right = jnp.bitwise_and(lanes_of(deep), half - 1) != half - 1
    low = lanes_of(chans) < half
    first = lanes_of(chans) == 0
    last = lanes_of(chans) == cols - 1
    none_deep = jnp.zeros((deep, cols), BF16)
    none = jnp.zeros((chans, cols), BF16)

    def norm_act(values, gain, keep):
        meansq = jnp.mean(values * values, axis=0, keepdims=True)
        y = values * (lax.rsqrt(meansq + 1e-06) * (0.5 * keep)) * gain
        return y + y * jnp.tanh(y)

    def put(ref, f, r, act):
        mid = act.astype(BF16)
        cross = pltpu.roll(mid, half, 1)
        left = jnp.where(first, none, jnp.where(low, pltpu.roll(mid, half + 1, 1), cross))
        right = jnp.where(last, none, jnp.where(low, cross, pltpu.roll(mid, half - 1, 1)))

        def store():
            for b, piece in enumerate((left, mid, right)):
                ref[f, r, pl.ds(b * chans, chans)] = piece
        return store

    def run(trips, *steps):
        for i in range(trips):
            for store in [store for step in steps for store in step(i)]:
                store()

    top_keep = jnp.where(t > 0, 1.0, 0.0)
    bottom_keep = jnp.where(t < tiles - 1, 1.0, 0.0)
    past_keep = jnp.where(s > 0, 1.0, 0.0)
    top_mask = jnp.full((deep, cols), top_keep, F32).astype(BF16)
    bottom_mask = jnp.full((deep, cols), bottom_keep, F32).astype(BF16)

    def row_keep(r, lo, hi):
        return top_keep if r < lo else bottom_keep if r >= hi else 1.0

    def windows(f, kind):
        def lines(q):
            got = cbuf[f, q]
            return got * top_mask if q == 0 else got * bottom_mask if q == 3 else got

        def between(q):
            one, two = lines(q), lines(q + 1)
            return (jnp.where(low_deep, pltpu.roll(one, half, 1), pltpu.roll(two, half, 1)),
                    jnp.where(low_deep, two, one))
        if kind < 2:
            here, (below, below_swap) = lines(kind), between(kind)
            swap = pltpu.roll(here, half, 1)
        elif kind == 2:
            here = below_swap = lines(2)
            swap = below = pltpu.roll(here, half, 1)
        else:
            (here, swap), below = between(2), lines(3)
            below_swap = pltpu.roll(below, half, 1)

        def to_left(v):
            return jnp.where(open_left, pltpu.roll(v, 1, 1), none_deep)

        def to_right(v):
            return jnp.where(open_right, pltpu.roll(v, cols - 1, 1), none_deep)
        even = jnp.concatenate([to_left(here), here, to_left(below), below], axis=0)
        odd = jnp.concatenate([swap, to_right(swap), below_swap, to_right(below_swap)], axis=0)
        return even, odd

    def grow(*jobs):
        cut = [windows(f, p) for f, p in jobs]
        even, odd = [jnp.dot(w[...], jnp.concatenate([c[k] for c in cut], axis=1), preferred_element_type=F32)
                     for k, w in enumerate((we, wo))]
        stores = []
        for k, (f, p) in enumerate(jobs):
            for phase in range(2):
                e = even[phase * chans:(phase + 1) * chans, k * cols:(k + 1) * cols] + vecs[0]
                o = odd[phase * chans:(phase + 1) * chans, k * cols:(k + 1) * cols] + vecs[0]
                for side in range(1 if p == 2 else 2):
                    r = 2 * ((0, 2, 4, 5)[p] + side) - 1 + phase
                    if 0 <= r < rows + 4:
                        if side == 0:
                            value = jnp.where(lanes_of(chans) < half, e, o).astype(BF16)
                        else:
                            value = pltpu.roll(jnp.where(lanes_of(chans) < half, o, e).astype(BF16), half, 1)

                        def store(f=f, r=r, value=value):
                            vals[f, r] = value
                        stores.append(store)
        return stores

    def growing(*works):
        return lambda i: grow(*works[i]) if i < len(works) else []

    def finish(f, r):
        keep = row_keep(r, 2, rows + 2)
        if f < frames:
            keep = keep * past_keep
        return put(x1, f, r, norm_act(vals[f, r].astype(F32), vecs[1], keep))

    inner = list(range(3, rows + 1))
    outer = [r for r in range(rows + 4) if r not in inner]

    def finishing(f, lines, trips):
        each = -(-len(lines) // trips)
        return lambda i: [finish(f, r) for r in lines[i * each:(i + 1) * each]]

    def conv(x, w, ends, mids_of, acc, f, newest_out, works, start_of, done):
        taps = [tap for tap in range(3) if 0 <= f - tap <= newest_out]
        lo, hi = taps[0], taps[-1] + 1
        part = pl.ds(lo * chans, (hi - lo) * chans)

        def dot(weights, rhs):
            return jnp.dot(weights, rhs, preferred_element_type=F32)

        def apart(pair):
            rhs = jnp.concatenate(
                [jnp.concatenate([x[f, r + a] for r in pair], axis=1) for a in range(3)], axis=0)
            got = dot(w[part], rhs)
            return [(r, got, j) for j, r in enumerate(pair)]

        def fours(*firsts):
            d = [jnp.concatenate([x[f, r + a, :full] for r in firsts], axis=1) for a in range(4)]
            e = [jnp.concatenate([x[f, r + a, full:] for r in firsts], axis=1) for a in range(4)]
            plus = dot(sums[mids_of, part], d[1] + d[2])
            minus = dot(sums[mids_of + 1, part], d[2] - d[1])
            even = dot(ends[0, part], jnp.concatenate([d[0] - d[2], e[0], e[1], e[2]], axis=0)) + (plus + minus)
            odd_row = dot(ends[1, part], jnp.concatenate([d[1] - d[3], e[1], e[2], e[3]], axis=0)) + (plus - minus)
            return [(r + k, got, j) for j, r in enumerate(firsts) for k, got in enumerate((even, odd_row))]

        def step(p):
            if p >= len(works):
                return []
            kind, rows_of = works[p]
            results = apart(rows_of) if kind == 0 else fours(*rows_of)

            def store():
                for tap in taps:
                    n = f - tap
                    totals = []
                    for r, got, j in results:
                        mine = got[(tap - lo) * chans:(tap - lo + 1) * chans, j * cols:(j + 1) * cols]
                        totals.append((r, mine + (start_of(n, r) if tap == 2 else acc[n, r])))
                    if tap == 0 and done is not None:
                        for k in range(0, len(totals), 2):
                            done(n, [r for r, _ in totals[k:k + 2]], [total for _, total in totals[k:k + 2]])
                    else:
                        for r, total in totals:
                            acc[n, r] = total
            return [store]
        return step

    mids = frames + 2

    early = [(1, (r, r + 2)) for r in range(3, rows - 1, 4)]
    late = [(1, (1, rows - 1)), (0, (0, rows + 1))]

    def conv_a(f, pairs=early + late):
        return conv(x1, w1, g1, 0, acc1, f, mids - 1, pairs, lambda n, r: vecs[2], None)

    def finished(n, pair, totals):
        flat = jnp.concatenate([total.astype(BF16) for total in totals], axis=1)
        wide = jnp.dot(flat, merge[...], preferred_element_type=F32)
        for j, r in enumerate(pair):
            spread[n % 2, pl.ds(r, chans, stride=rows)] = wide[:, j * cols:(j + 1) * cols]

    leaving = [pltpu.make_async_copy(staged.at[n], out.at[:, n], leave.at[n]) for n in range(frames)]

    def emit(n):
        staged[n] = spread[n % 2].reshape(chans, rows, cols).astype(BF16)
        leaving[n].start()

    def conv_b(f):
        return conv(x2, None, g2, 2, acc2, f, frames - 1, [(1, (r, r + 2)) for r in range(0, rows, 4)], lambda n, r: vals[frames + n, r + 2].astype(F32) + vecs[4], finished)

    def second(n, r):
        keep = row_keep(r, 1, rows + 1)
        if n < 2:
            keep = keep * past_keep
        return put(x2, n, r, norm_act(acc1[n, r], vecs[3], keep))

    def second_two(n):
        return lambda p: [second(n, 2 * p), second(n, 2 * p + 1)] if 2 * p < rows + 2 else []

    def arrived(f):
        to_cross[f - frames].wait_recv()
        to_mate[f - frames].wait_recv()

    def hops(f):
        return [hop_mate[f]] if f < wide_far else [hop_up[f], hop_down[f]]

    def relay(*sent):
        for f in sent:
            far[f].wait_recv()
            for copy in hops(f):
                copy.start()

    def landed(*sent):
        for f in sent:
            for copy in hops(f):
                copy.wait_recv()

    def middle(f):
        return growing(((f, 1), (f, 2)))

    def rim(f):
        return growing(((f, 0), (f, 3)))

    wide_pairs = (rows + 2) // 2
    lines = list(range(rows + 4))
    n = 2 * frames
    run(1, middle(n - 1))
    run(1, middle(n - 2), finishing(n - 1, inner, 1))
    run(2, middle(n - 3), conv_a(n - 1, early), finishing(n - 2, inner, 2))
    run(2, middle(n - 4), conv_a(n - 2, early), finishing(n - 3, inner, 2))
    run(2, conv_a(n - 3, early), finishing(n - 4, inner, 2))
    run(2, conv_a(n - 4, early))
    def rims(f, *others):
        run(1, rim(f), *others)

    arrived(n - 1)
    arrived(n - 2)
    rims(n - 1)
    rims(n - 2, finishing(n - 1, outer, 1))
    run(3, conv_a(n - 1, late), finishing(n - 2, outer, 3))
    arrived(n - 3)
    arrived(n - 4)
    far_go(0)
    pl.when(has_prev)(lambda: relay(3))
    rims(n - 3)
    run(3, conv_a(n - 2, late), finishing(n - 3, outer, 3), rim(n - 4))
    run(3, conv_a(n - 3, late), finishing(n - 4, outer, 3))
    pl.when(has_prev)(lambda: relay(2))
    run(wide_pairs, conv_a(n - 4, late), second_two(5), middle(3))
    run(wide_pairs, second_two(4), conv_b(5), finishing(3, inner, 2), middle(2))
    run(4, conv_b(4), conv_a(3, early), finishing(2, inner, 3))
    run(3, conv_a(2, early))

    @pl.when(has_prev)
    def _():
        landed(3)
        relay(1)
    run(2, rim(3), middle(1))
    run(3, finishing(3, outer, 3), finishing(1, inner, 3))
    run(3, conv_a(3, late), conv_a(1, early))
    run(wide_pairs, second_two(3))
    run(4, conv_b(3))

    @pl.when(has_prev)
    def _():
        relay(0)
        landed(2, 1)
    run(1, rim(2))
    emit(3)
    run(3, rim(1), finishing(2, outer, 3))
    run(3, conv_a(2, late), middle(0), finishing(1, outer, 3))
    run(wide_pairs, second_two(2), conv_a(1, late), finishing(0, inner, 3))
    run(4, conv_b(2), conv_a(0, early))
    emit(2)
    pl.when(has_prev)(lambda: landed(0))
    run(1, rim(0))
    run(wide_pairs, finishing(0, outer, 3), second_two(1))
    run(wide_pairs, conv_a(0, late))
    run(wide_pairs, conv_b(1), second_two(0))
    emit(1)
    run(4, conv_b(0))
    emit(0)

    for f in range(frames):
        leaving[f].wait()
        pl.when(has_next)(far[f].wait_send)
        for copy in (to_cross[f], to_mate[f]):
            copy.wait_send()
        for copy in hops(f):
            pl.when(has_prev)(copy.wait_send)


def shards(slabs, tiles, coarse, up_weight, up_bias, gain_one, conv_one, bias_one, gain_two, conv_two, bias_two):
    deep, frames, lines, half = coarse.shape
    chans = up_weight.shape[2]
    rows, cols = 2 * lines, 2 * half
    native = coarse.transpose(1, 2, 3, 0).reshape(frames, lines * half, deep)
    row = lambda vec: vec.reshape(1, chans)
    vmem = pl.BlockSpec(memory_space=pltpu.VMEM)
    far_away = pl.BlockSpec(memory_space=pl.ANY)
    return pl.pallas_call(
        functools.partial(body, slabs, tiles),
        out_shape=jax.ShapeDtypeStruct((chans, frames, rows, cols), BF16),
        in_specs=[far_away] * 4 + [vmem] * 5,
        out_specs=far_away,
        scratch_shapes=[
            pltpu.VMEM((frames, lines * half, deep), BF16),
            pltpu.VMEM((2 * frames, 4, deep, cols), BF16),
            pltpu.VMEM((2 * chans, 4 * deep), BF16),
            pltpu.VMEM((2 * chans, 4 * deep), BF16),
            pltpu.VMEM((3 * chans, 9 * chans), BF16),
            pltpu.VMEM((2, 3 * chans, 3 * chans // 256 * 256 + chans), BF16),
            pltpu.VMEM((4, 3 * chans, 3 * chans // 256 * 256), BF16),
            pltpu.VMEM((2, 3 * chans, 3 * chans // 256 * 256 + chans), BF16),
            pltpu.VMEM((5, chans, cols), F32),
            pltpu.VMEM((2 * cols, 2 * cols), BF16),
            pltpu.VMEM((2 * frames, rows + 4, chans, cols), BF16),
            pltpu.VMEM((2 * frames, rows + 4, 3 * chans, cols), BF16),
            pltpu.VMEM((frames + 2, rows + 2, chans, cols), F32),
            pltpu.VMEM((frames + 2, rows + 2, 3 * chans, cols), BF16),
            pltpu.VMEM((frames, rows, chans, cols), F32),
            pltpu.VMEM(up_weight.shape, BF16),
            pltpu.VMEM(conv_one.shape, BF16),
            pltpu.VMEM(conv_two.shape, BF16),
            pltpu.VMEM((2, chans * rows, cols), F32),
            pltpu.VMEM((frames, chans, rows, cols), BF16),
            pltpu.SemaphoreType.DMA((frames,)),
            pltpu.SemaphoreType.DMA((3,)),
            pltpu.SemaphoreType.DMA((frames,)),
            pltpu.SemaphoreType.DMA((frames, 2)),
            pltpu.SemaphoreType.DMA((frames, 2)),
            pltpu.SemaphoreType.DMA((frames,)),
            pltpu.SemaphoreType.DMA((frames,)),
            pltpu.SemaphoreType.DMA((frames, 2)),
            pltpu.SemaphoreType.DMA((frames, 2)),
        ],
        compiler_params=pltpu.CompilerParams(collective_id=0, has_side_effects=True, vmem_limit_bytes=60 * 2**20),
    )(native, up_weight, conv_one, conv_two, row(up_bias), row(gain_one), row(bias_one), row(gain_two), row(bias_two))


def solution(mesh):
    return jax.shard_map(
        functools.partial(shards, mesh.shape["slab"], mesh.shape["tile"]),
        mesh=mesh,
        in_specs=(P(None, "slab", "tile", None), P(), P(), P(), P(), P(), P(), P(), P()),
        out_specs=P(None, "slab", "tile", None),
        check_vma=False,
    )
```
